32 devices in a mesh: tm: 8 (over z, x), pix: 4 (over y, core).
Axes of the slice: x: 2, y: 2, z: 4, core: 2. Of those that a mesh axis runs over, the one named last changes fastest.
Arguments:
- movie: bfloat16 [8, 2048, 2048], P('tm', 'pix'), may hold values from -6 to 6
- shifts: int32 [8, 16, 16, 2], P('tm', 'pix'), may hold values from -16 to 16
- footprints: bfloat16 [4, 256, 64, 4096], P('pix', 'tm'), may hold values from -0.0234375 to 0.0234375
- neuron_ids: int32 [4, 256, 64], P('pix', 'tm'), may hold values from 0 to 4095
Outputs:
- traces: float32 [4096, 8], P(('tm', 'pix'))
The draws below stay inside these ranges and needn't reach their ends.
All inputs are finite; a program needn't handle non-finite values.
Results may differ from the reference program's by a relative error of at most 0.0029.
Values may be sent and summed in bfloat16 or wider, within the bound.
A program may use at most 128 MiB of HBM per device.

```python
import jax
import jax.numpy as jnp
from jax import lax

HEIGHT = 2048
WIDTH = 2048
TILE = 128
MAXSHIFT = 16
PATCH = 64
FOOT_COLS = 64
HOMES = 4
FRAMES = 8
PATCHES = 1024
NEURONS = 4096
N_PIX = 4


def draw_neuron_ids(key, part):
    rows_p = HEIGHT // PATCH
    cols_p = WIDTH // PATCH
    count = rows_p * cols_p
    key_rows, key_cols, key_home, key_far, key_pick = jax.random.split(key, 5)
    step_rows = jax.random.randint(key_rows, (count, FOOT_COLS), -1, 2)
    step_cols = jax.random.randint(key_cols, (count, FOOT_COLS), -1, 2)
    homes = jax.random.randint(key_home, (count, FOOT_COLS), 0, HOMES)
    far_labels = jax.random.randint(key_far, (count, FOOT_COLS), 0, NEURONS)
    far_pick = jax.random.randint(key_pick, (count, FOOT_COLS), 0, 4)
    places = jnp.arange(count, dtype=jnp.int32)
    target_rows = jnp.clip(places[:, None] // cols_p + step_rows, 0, rows_p - 1)
    target_cols = jnp.clip(places[:, None] % cols_p + step_cols, 0, cols_p - 1)
    near_labels = (target_rows * cols_p + target_cols) * HOMES + homes
    labels = jnp.where(far_pick == 0, far_labels, near_labels)
    labels = labels.at[0, 0].set(0)
    labels = labels.at[count - 1, 0].set(NEURONS - 1)
    return labels.astype(jnp.int32).reshape(N_PIX, count // N_PIX, FOOT_COLS)


def set_ends(array, stream_key, least, high):
    extent = array.shape
    place = [jax.random.randint(jax.random.fold_in(stream_key, axis), (), 0, extent[axis]) for axis in range(len(extent))]
    array = array.at[tuple(place)].set(least)
    longest = extent.index(max(extent))
    place[longest] = (place[longest] + 1) % extent[longest]
    return array.at[tuple(place)].set(high)


def levels(rng, dims, cuts, least, largest):
    level = 1.0
    for position, parts in cuts:
        draws = jax.random.uniform(jax.random.fold_in(jax.random.fold_in(rng, 6), position), (parts,), jnp.float32, least / len(cuts), largest / len(cuts))
        level = level * jnp.repeat(jnp.exp(draws), dims[position] // parts).reshape((-1,) + (1,) * (len(dims) - 1 - position))
    return level


def gaussian(rng, extent, scale, bound, cuts=(), kind=jnp.bfloat16):
    result = jax.random.normal(rng, extent, jnp.float32) * scale
    if len(cuts) > 0:
        result = levels(rng, extent, cuts, -0.22, 0.18) * result
    return jnp.clip(result, min=-bound, max=bound).astype(kind)


def setup_inputs(seed: int = 0) -> dict:
    seeds = jax.random.split(jax.random.key(seed), 5)
    return {
        "movie": gaussian(seeds[0], (FRAMES, HEIGHT, WIDTH), 1.0, 6.0, ((0, 8), (1, 4))),
        "shifts": set_ends(jax.random.randint(seeds[1], (FRAMES, HEIGHT // TILE, WIDTH // TILE, 2), 0 - MAXSHIFT, MAXSHIFT + 1), jax.random.fold_in(seeds[1], 1), 0 - MAXSHIFT, MAXSHIFT).astype(jnp.int32),
        "footprints": gaussian(seeds[2], (N_PIX, PATCHES // N_PIX, FOOT_COLS, PATCH * PATCH), (16 * PATCH * PATCH) ** -0.5, 0.0234375, ((0, 4), (1, 8))),
        "neuron_ids": draw_neuron_ids(jax.random.fold_in(seeds[4], 71), 0),
    }


pixel_sigma = 3.0
frame_sigma = 4.0


def gauss_table(count, sigma):
    places = jnp.arange(count).astype(jnp.float32)
    apart = places[:, None] - places[None, :]
    weights = jnp.exp(-apart * apart / (2.0 * sigma * sigma))
    return weights / jnp.sum(weights, axis=1, keepdims=True)


def rounded(values):
    return lax.optimization_barrier(values.astype(jnp.bfloat16)).astype(jnp.float32)


def shift_frame(frame, shift):
    padded = jnp.pad(frame, MAXSHIFT)
    row_index = jnp.arange(HEIGHT, dtype=jnp.int32)[:, None] + jnp.zeros((1, WIDTH), jnp.int32)
    col_index = jnp.arange(WIDTH, dtype=jnp.int32)[None, :] + jnp.zeros((HEIGHT, 1), jnp.int32)
    vertical = shift[row_index // TILE, col_index // TILE, 0]
    horizontal = shift[row_index // TILE, col_index // TILE, 1]
    return padded[row_index + MAXSHIFT + vertical, col_index + MAXSHIFT + horizontal]


def reference(movie, shifts, footprints, neuron_ids):
    registered = lax.map(lambda pair: shift_frame(pair[0], pair[1]), (movie, shifts))
    patch_table = rounded(gauss_table(PATCH, pixel_sigma))
    time_table = rounded(gauss_table(FRAMES, frame_sigma))
    rows_p = HEIGHT // PATCH
    cols_p = WIDTH // PATCH
    blocks = footprints.reshape(rows_p, cols_p, FOOT_COLS, PATCH, PATCH)

    def one_row(item):
        index, foot_block = item
        strip = lax.dynamic_slice_in_dim(registered, index * PATCH, PATCH, axis=1)
        pixels = strip.reshape(FRAMES, PATCH, cols_p, PATCH).astype(jnp.float32)
        along_rows = rounded(jnp.einsum("ij,fjbc->fibc", patch_table, pixels))
        along_cols = rounded(jnp.einsum("fibj,cj->fibc", along_rows, patch_table))
        along_time = jnp.einsum("gf,fibc->gibc", time_table, along_cols)
        cleaned = rounded(pixels - along_time)
        return jnp.einsum("fibc,bkic->bkf", cleaned, foot_block.astype(jnp.float32))

    partials = lax.map(one_row, (jnp.arange(rows_p, dtype=jnp.int32), blocks))
    partials = partials.reshape(PATCHES * FOOT_COLS, FRAMES)
    return jax.ops.segment_sum(partials, neuron_ids.reshape(-1), num_segments=NEURONS)
```

```python
import jax
import jax.numpy as jnp
import ml_dtypes
import numpy as np
from jax import lax
from jax.experimental import pallas as pl
from jax.experimental.pallas import tpu as pltpu
from jax.sharding import PartitionSpec as P

TILE = 128
MAXSHIFT = 16
PATCH = 64
NEURONS = 4096
LANES = 128
GROUP = 4
EARLY = 2


pixel_sigma = 3.0
frame_sigma = 4.0


def gauss_table(count, sigma):
    places = np.arange(count).astype(np.float32)
    apart = places[:, None] - places[None, :]
    weights = np.exp(-apart * apart / np.float32(2.0 * sigma * sigma)).astype(np.float32)
    table = weights / np.sum(weights, axis=1, keepdims=True, dtype=np.float32)
    return table.astype(ml_dtypes.bfloat16)


def halo(band):
    count = lax.axis_size("pix")
    up = [(i, i + 1) for i in range(count - 1)]
    down = [(i + 1, i) for i in range(count - 1)]
    before = lax.ppermute(band[-MAXSHIFT:], "pix", up)
    after = lax.ppermute(band[:MAXSHIFT], "pix", down)
    return before, after


def register_kernel(shift_ref, band_ref, before_ref, after_ref, out_ref, padded):
    rows, width = band_ref.shape
    across = width // TILE
    tall = rows + 2 * MAXSHIFT
    for j in (0, across + 1):
        padded[j] = jnp.zeros((tall, TILE), jnp.float32)
    for j in range(across):
        lanes = pl.ds(j * TILE, TILE)
        padded[j + 1, pl.ds(0, MAXSHIFT), :] = before_ref[:, lanes].astype(jnp.float32)
        padded[j + 1, pl.ds(MAXSHIFT, rows), :] = band_ref[:, lanes].astype(jnp.float32)
        padded[j + 1, pl.ds(rows + MAXSHIFT, MAXSHIFT), :] = after_ref[:, lanes].astype(jnp.float32)

    gap = lax.broadcasted_iota(jnp.int32, (2 * TILE, TILE), 0) - lax.broadcasted_iota(
        jnp.int32, (2 * TILE, TILE), 1
    )

    @pl.loop(0, rows // TILE)
    def _(a):
        for b in range(across):
            place = (a * across + b) * 2
            dy = shift_ref[place]
            dx = shift_ref[place + 1]
            left = dx < 0
            start = jnp.where(left, b, b + 1)
            at = pl.ds(a * TILE + MAXSHIFT + dy, TILE)
            window = jnp.concatenate([padded[start, at, :], padded[start + 1, at, :]], axis=1)
            pick = (gap == jnp.where(left, dx + TILE, dx)).astype(jnp.float32).astype(jnp.bfloat16)
            moved = jnp.dot(window.astype(jnp.bfloat16), pick, preferred_element_type=jnp.float32)
            out_ref[pl.ds(pl.multiple_of(a * TILE, TILE), TILE), b * TILE : (b + 1) * TILE] = moved.astype(
                jnp.bfloat16
            )


def register(band, before, after, shifts):
    rows, width = band.shape
    vmem = pl.BlockSpec(memory_space=pltpu.VMEM)
    return pl.pallas_call(
        register_kernel,
        out_shape=jax.ShapeDtypeStruct((rows, width), jnp.bfloat16),
        in_specs=[pl.BlockSpec(memory_space=pltpu.SMEM), vmem, vmem, vmem],
        out_specs=vmem,
        scratch_shapes=[pltpu.VMEM((width // TILE + 2, rows + 2 * MAXSHIFT, TILE), jnp.float32)],
        compiler_params=pltpu.CompilerParams(vmem_limit_bytes=24 << 20),
        name="register",
    )(shifts.reshape(-1), band, before, after)


def project_step(local, x, blocks, ids, row_ref, col_ref, mix_ref):
    frames, side, cols = x.shape
    foot_cols = blocks.shape[1]
    half = row_ref.shape[0] // frames
    moved = x.reshape(frames * side, cols)
    chunk = row_ref.shape[0]
    along_rows = jnp.concatenate(
        [
            jnp.dot(row_ref[...], moved[i : i + chunk], preferred_element_type=jnp.float32)
            for i in range(0, frames * side, chunk)
        ],
        axis=0,
    ).astype(jnp.bfloat16)
    along_cols = jnp.dot(along_rows, col_ref[...], preferred_element_type=jnp.float32).astype(jnp.bfloat16)
    patches = cols // side
    low = lax.broadcasted_iota(jnp.int32, (frames, LANES), 1) < side
    pieces = [[] for _ in range(patches)]
    for h in range(side // half):
        stack = [moved[f * side + h * half : f * side + (h + 1) * half] for f in range(frames)]
        stack += [along_cols[f * side + h * half : f * side + (h + 1) * half] for f in range(frames)]
        clean = jnp.dot(mix_ref[...], jnp.concatenate(stack, axis=0), preferred_element_type=jnp.float32)
        for i in range(half // 2):
            for j in range(cols // LANES):
                first = clean[2 * i * frames : (2 * i + 1) * frames, j * LANES : (j + 1) * LANES]
                second = clean[(2 * i + 1) * frames : (2 * i + 2) * frames, j * LANES : (j + 1) * LANES]
                pieces[2 * j].append(jnp.where(low, first, pltpu.roll(second, side, 1)))
                pieces[2 * j + 1].append(jnp.where(low, pltpu.roll(first, side, 1), second))
    pixels = jnp.concatenate([jnp.concatenate(p, axis=1) for p in pieces], axis=0).astype(jnp.bfloat16)
    blocks = blocks.reshape(patches * foot_cols, side * side)
    product = lax.dot_general(pixels, blocks, (((1,), (1,)), ((), ())), preferred_element_type=jnp.float32)
    count = product.shape[1]
    owner_patch = lax.broadcasted_iota(jnp.int32, (frames, count), 1) // foot_cols
    partial = jnp.zeros((frames, count), jnp.float32)
    for p in range(patches):
        partial = jnp.where(owner_patch == p, product[p * frames : (p + 1) * frames], partial)
    owner = jnp.broadcast_to(ids // local, (frames, count))
    within = ids % local
    onehot = (
        (lax.broadcasted_iota(jnp.int32, (local, count), 0) == within).astype(jnp.float32).astype(jnp.bfloat16)
    )
    owner_order = list(range(0, NEURONS // local, 2)) + list(range(1, NEURONS // local, 2))
    total = None
    rest = partial
    for _ in range(3):
        piece = rest.astype(jnp.bfloat16).astype(jnp.float32)
        rest = rest - piece
        spread = jnp.concatenate(
            [jnp.where(owner == o, piece, 0.0) for o in owner_order], axis=0
        ).astype(jnp.bfloat16)
        term = lax.dot_general(spread, onehot, (((1,), (1,)), ((), ())), preferred_element_type=jnp.float32)
        total = term if total is None else total + term
    return total


def fused_kernel(
    local,
    shift_ref,
    movie_ref,
    foot_ref,
    ids_ref,
    row_hbm,
    col_hbm,
    mix_hbm,
    out_ref,
    band,
    before,
    after,
    padded,
    slabs,
    moved,
    feet,
    row_ref,
    col_ref,
    mix_ref,
    labels,
    sums,
    other,
    kept,
    landed,
    load,
    table,
    feed,
    halo_send,
    halo_recv,
    send,
    recv,
    here,
    pair_send,
    pair_recv,
    last_send,
    last_recv,
):
    groups, side, width = slabs.shape
    steps = feet.shape[0]
    wide = width // steps
    rows = band.shape[0]
    across = width // TILE
    me = lax.axis_index("tm")
    pix = lax.axis_index("pix")
    bands = lax.axis_size("pix")
    half = groups // 2
    upper = me // half
    mesh_id = pl.DeviceIdType.MESH

    barrier = pltpu.get_barrier_semaphore()
    for d in range(1, groups):
        pl.semaphore_signal(barrier, inc=1, device_id={"tm": lax.rem(me + d, groups)}, device_id_type=mesh_id)
    for d in range(1, bands):
        pl.semaphore_signal(barrier, inc=1, device_id={"pix": lax.rem(pix + d, bands)}, device_id_type=mesh_id)

    inner = TILE - MAXSHIFT
    parts = ((inner, rows - inner), (0, inner), (rows - inner, rows))

    def load_copy(i):
        first, last = parts[i]
        at = pl.ds(first, last - first)
        return pltpu.make_async_copy(movie_ref.at[at], band.at[at], load.at[i])

    table_copies = [
        pltpu.make_async_copy(src, dst, table.at[i])
        for i, (src, dst) in enumerate(((row_hbm, row_ref), (col_hbm, col_ref), (mix_hbm, mix_ref)))
    ]

    def feet_copy(s):
        return pltpu.make_async_copy(foot_ref.at[pl.ds(s * GROUP, GROUP)], feet.at[s], feed.at[s])

    for i in range(3):
        load_copy(i).start()
    for copy in table_copies:
        copy.start()

    tall = rows + 2 * MAXSHIFT
    for j in (0, across + 1):
        padded[j] = jnp.zeros((tall, TILE), jnp.float32)

    def widen(i):
        first, last = parts[i]
        for j in range(across):
            lanes = pl.ds(j * TILE, TILE)
            padded[j + 1, pl.ds(first + MAXSHIFT, last - first), :] = band[first:last, lanes].astype(jnp.float32)

    gap = lax.broadcasted_iota(jnp.int32, (2 * TILE, TILE), 0) - lax.broadcasted_iota(
        jnp.int32, (2 * TILE, TILE), 1
    )

    def register_row(a):
        for b in range(across):
            dy = shift_ref[a, 0, b]
            dx = shift_ref[a, 1, b]
            left = dx < 0
            start = jnp.where(left, b, b + 1)
            at = pl.ds(a * TILE + MAXSHIFT + dy, TILE)
            window = jnp.concatenate([padded[start, at, :], padded[start + 1, at, :]], axis=1)
            pick = (gap == jnp.where(left, dx + TILE, dx)).astype(jnp.float32).astype(jnp.bfloat16)
            tile = jnp.dot(window.astype(jnp.bfloat16), pick, preferred_element_type=jnp.float32)
            slabs[pl.ds(2 * a, 2), :, b * TILE : (b + 1) * TILE] = tile.astype(jnp.bfloat16).reshape(2, side, TILE)

    def tile_row(i):
        up = jnp.where(i == 0, 1, jnp.where(i == 1, 2, jnp.where(i == 2, 0, 3)))
        return jnp.where(upper == 1, up, 3 - up)

    def send_copy(s, to):
        d = lax.rem(to - me + groups, groups)
        lanes = pl.ds(pl.multiple_of(s * wide, wide), wide)
        return pltpu.make_async_remote_copy(
            src_ref=slabs.at[to, :, lanes],
            dst_ref=moved.at[me, :, lanes],
            send_sem=send.at[s, d - 1],
            recv_sem=recv.at[s, d - 1],
            device_id={"tm": to},
            device_id_type=mesh_id,
        )

    def halo_copy(i):
        source = (rows - MAXSHIFT, 0)[i]
        return pltpu.make_async_remote_copy(
            src_ref=movie_ref.at[pl.ds(source, MAXSHIFT)],
            dst_ref=(before, after)[i],
            send_sem=halo_send.at[i],
            recv_sem=halo_recv.at[i],
            device_id={"pix": (pix + 1, pix - 1)[i]},
            device_id_type=mesh_id,
        )

    sends_halo = (pix < bands - 1, pix > 0)
    gets_halo = (pix > 0, pix < bands - 1)

    load_copy(0).wait()
    widen(0)
    nearest = tile_row(0)
    register_row(nearest)

    pl.semaphore_wait(barrier, groups + bands - 2)

    for i in range(2):

        @pl.when(sends_halo[i])
        def _():
            halo_copy(i).start()

    @pl.loop(0, EARLY)
    def _(s):
        for e in range(2):
            send_copy(s, 2 * nearest + e).start()

    @pl.loop(1, 4)
    def _(i):
        @pl.when(i == 2)
        def _():
            for k in (1, 2):
                load_copy(k).wait()
                widen(k)
            for k in range(2):

                @pl.when(gets_halo[k])
                def _():
                    halo_copy(k).wait_recv()

                @pl.when(jnp.logical_not(gets_halo[k]))
                def _():
                    (before, after)[k][...] = jnp.zeros((MAXSHIFT, width), jnp.bfloat16)

            for j in range(across):
                lanes = pl.ds(j * TILE, TILE)
                padded[j + 1, pl.ds(0, MAXSHIFT), :] = before[:, lanes].astype(jnp.float32)
                padded[j + 1, pl.ds(rows + MAXSHIFT, MAXSHIFT), :] = after[:, lanes].astype(jnp.float32)

        register_row(tile_row(i))

    own = pltpu.make_async_copy(slabs.at[me], moved.at[me], here)
    own.start()
    spot = lax.rem(me, half)
    targets = [(1 - upper) * half + lax.rem(spot + e, half) for e in range(half)]
    targets += [upper * half + lax.rem(spot + e, half) for e in range(1, half)]

    @pl.loop(0, steps)
    def _(s):
        for to in targets:

            @pl.when(jnp.logical_or(s >= EARLY, to // 2 != nearest))
            def _():
                send_copy(s, to).start()

    @pl.loop(0, steps)
    def _(s):
        feet_copy(s).start()

    sums[...] = jnp.zeros_like(sums)
    for s in range(steps):
        labels[s] = jnp.concatenate([ids_ref[p : p + 1, :] for p in range(s * GROUP, (s + 1) * GROUP)], axis=1)
    for copy in table_copies:
        copy.wait()
    own.wait()

    @pl.loop(0, steps)
    def _(s):
        feet_copy(s).wait()
        for to in targets:
            send_copy(s, to).wait_recv()
        lanes = pl.ds(pl.multiple_of(s * wide, wide), wide)
        sums[...] += project_step(local, moved[:, :, lanes], feet[s], labels[s], row_ref, col_ref, mix_ref)

    frames = groups
    core = lax.rem(pix, 2)
    count = groups * bands // 2
    block = count * frames
    pair_copy = pltpu.make_async_remote_copy(
        src_ref=sums.at[pl.ds(pl.multiple_of((1 - core) * block, block), block)],
        dst_ref=other,
        send_sem=pair_send,
        recv_sem=pair_recv,
        device_id={"pix": pix + 1 - 2 * core},
        device_id_type=mesh_id,
    )
    pair_copy.start()
    pair_copy.wait_recv()
    kept[...] = sums[pl.ds(pl.multiple_of(core * block, block), block), :] + other[...]
    place = me * (bands // 2) + pix // 2

    def last_copy(d):
        to = lax.rem(place + d, count)
        return pltpu.make_async_remote_copy(
            src_ref=kept.at[pl.ds(pl.multiple_of(to * frames, frames), frames)],
            dst_ref=landed.at[place],
            send_sem=last_send.at[d - 1],
            recv_sem=last_recv.at[d - 1],
            device_id={"tm": to // (bands // 2), "pix": lax.rem(to, bands // 2) * 2 + core},
            device_id_type=mesh_id,
        )

    for d in range(1, count):
        last_copy(d).start()
    landed[place] = kept[pl.ds(pl.multiple_of(place * frames, frames), frames), :]
    for d in range(1, count):
        last_copy(d).wait_recv()
    out_ref[...] = jnp.sum(landed[...], axis=0)

    for i in range(2):

        @pl.when(sends_halo[i])
        def _():
            halo_copy(i).wait_send()

    @pl.loop(0, steps)
    def _(s):
        for to in targets:
            send_copy(s, to).wait_send()

    pair_copy.wait_send()
    for d in range(1, count):
        last_copy(d).wait_send()


def fused(band, shifts, footprints, ids, groups, bands):
    rows, width = band.shape
    frames = groups
    owners = groups * bands
    steps = width // (GROUP * PATCH)
    foot_cols = footprints.shape[1]
    local = NEURONS // owners
    base = gauss_table(PATCH, pixel_sigma)
    time = gauss_table(frames, frame_sigma)
    full = GROUP * PATCH
    eye = np.eye(GROUP, dtype=np.float32)
    row_table = np.kron(eye, base.astype(np.float32)).astype(ml_dtypes.bfloat16)
    col_table = np.kron(eye, base.astype(np.float32).T).astype(ml_dtypes.bfloat16)
    half = full // frames
    spots = np.eye(half, dtype=np.float32)
    keep = np.einsum("gf,rs->rgfs", np.eye(frames, dtype=np.float32), spots)
    blur = np.einsum("gf,rs->rgfs", time.astype(np.float32), spots)
    mix = np.concatenate([keep.reshape(full, full), -blur.reshape(full, full)], axis=1).astype(ml_dtypes.bfloat16)
    vmem = pl.BlockSpec(memory_space=pltpu.VMEM)
    hbm = pl.BlockSpec(memory_space=pltpu.HBM)
    tall = rows + 2 * MAXSHIFT
    bf16, f32, dma = jnp.bfloat16, jnp.float32, pltpu.SemaphoreType.DMA
    count = owners // 2
    return pl.pallas_call(
        lambda *refs: fused_kernel(local, *refs),
        out_shape=jax.ShapeDtypeStruct((frames, local), f32),
        in_specs=[pl.BlockSpec(memory_space=pltpu.SMEM), hbm, hbm, vmem, hbm, hbm, hbm],
        out_specs=vmem,
        scratch_shapes=[
            pltpu.VMEM((rows, width), bf16),
            pltpu.VMEM((MAXSHIFT, width), bf16),
            pltpu.VMEM((MAXSHIFT, width), bf16),
            pltpu.VMEM((width // TILE + 2, tall, TILE), f32),
            pltpu.VMEM((groups, PATCH, width), bf16),
            pltpu.VMEM((groups, PATCH, width), bf16),
            pltpu.VMEM((steps, GROUP, foot_cols, PATCH * PATCH), bf16),
            pltpu.VMEM(row_table.shape, bf16),
            pltpu.VMEM(col_table.shape, bf16),
            pltpu.VMEM(mix.shape, bf16),
            pltpu.VMEM((steps, 1, GROUP * foot_cols), jnp.int32),
            pltpu.VMEM((owners * frames, local), f32),
            pltpu.VMEM((count * frames, local), f32),
            pltpu.VMEM((count * frames, local), f32),
            pltpu.VMEM((count, frames, local), f32),
            dma((3,)),
            dma((3,)),
            dma((steps,)),
            dma((2,)),
            dma((2,)),
            dma((steps, groups - 1)),
            dma((steps, groups - 1)),
            dma,
            dma,
            dma,
            dma((count - 1,)),
            dma((count - 1,)),
        ],
        compiler_params=pltpu.CompilerParams(
            vmem_limit_bytes=60 << 20, collective_id=0, has_side_effects=True
        ),
        name="fused",
    )(
        shifts,
        band,
        footprints,
        ids,
        jnp.asarray(row_table),
        jnp.asarray(col_table),
        jnp.asarray(mix),
    )


def project_general(moved, footprints, labels, owners):
    frames, side, width = moved.shape
    base = jnp.asarray(gauss_table(side, pixel_sigma))
    time = jnp.asarray(gauss_table(frames, frame_sigma))
    blocks = moved.reshape(frames, side, width // side, side)
    dot = lambda spec, a, b: jnp.einsum(spec, a, b, preferred_element_type=jnp.float32)
    along_rows = dot("ij,fjpc->fipc", base, blocks).astype(jnp.bfloat16)
    along_cols = dot("fipc,dc->fipd", along_rows, base).astype(jnp.bfloat16)
    clean = (blocks.astype(jnp.float32) - dot("gf,fipc->gipc", time, along_cols)).astype(jnp.bfloat16)
    pixels = clean.transpose(2, 0, 1, 3).reshape(width // side, frames, side * side)
    partial = dot("pfx,pkx->fpk", pixels, footprints).reshape(frames, -1)
    wanted = jnp.arange(NEURONS, dtype=jnp.int32)
    onehot = (labels.reshape(-1)[:, None] == wanted[None, :]).astype(jnp.float32)
    sums = jnp.dot(partial, onehot, precision=lax.Precision.HIGHEST, preferred_element_type=jnp.float32)
    return sums.reshape(frames, owners, -1).transpose(1, 0, 2).reshape(owners * frames, -1)


def on_device(movie, shifts, footprints, neuron_ids):
    band = movie[0]
    rows, width = band.shape
    groups = lax.axis_size("tm")
    bands = lax.axis_size("pix")
    owners = groups * bands
    wide = footprints.shape[1] * PATCH
    frames = groups * movie.shape[0]
    fits = (
        frames == groups
        and rows == 4 * TILE
        and rows == groups * PATCH
        and frames * 32 == GROUP * PATCH
        and wide == width
        and bands % 2 == 0
        and NEURONS // owners == LANES
    )
    if fits:
        return fused(band, shifts[0].transpose(0, 2, 1), footprints[0], neuron_ids[0], groups, bands).T
    before, after = halo(band)
    registered = register(band, before, after, shifts)
    slabs = registered.reshape(rows // PATCH, PATCH, width // wide, wide)
    slabs = slabs.transpose(0, 2, 1, 3).reshape(groups, PATCH, wide)
    moved = lax.all_to_all(slabs, "tm", split_axis=0, concat_axis=0, tiled=True)
    sums = project_general(moved, footprints[0], neuron_ids[0], owners)
    sums = lax.all_to_all(
        sums.reshape(owners, frames, -1), ("tm", "pix"), split_axis=0, concat_axis=0, tiled=True
    )
    return jnp.sum(sums, axis=0).T


def solution(mesh):
    in_specs = (
        P("tm", "pix", None),
        P("tm", "pix", None, None),
        P("pix", "tm", None, None),
        P("pix", "tm", None),
    )
    out_specs = P(("tm", "pix"), None)
    return jax.shard_map(
        on_device, mesh=mesh, in_specs=in_specs, out_specs=out_specs, check_vma=False
    )
```

```python
import jax
import jax.numpy as jnp
import ml_dtypes
import numpy as np
from jax import lax
from jax.experimental import pallas as pl
from jax.experimental.pallas import tpu as pltpu
from jax.sharding import PartitionSpec as P

TILE = 128
MAXSHIFT = 16
PATCH = 64
NEURONS = 4096
LANES = 128
GROUP = 4
EARLY = 2


pixel_sigma = 3.0
frame_sigma = 4.0


def gauss_table(count, sigma):
    places = np.arange(count).astype(np.float32)
    apart = places[:, None] - places[None, :]
    weights = np.exp(-apart * apart / np.float32(2.0 * sigma * sigma)).astype(np.float32)
    table = weights / np.sum(weights, axis=1, keepdims=True, dtype=np.float32)
    return table.astype(ml_dtypes.bfloat16)


def halo(band):
    count = lax.axis_size("pix")
    up = [(i, i + 1) for i in range(count - 1)]
    down = [(i + 1, i) for i in range(count - 1)]
    before = lax.ppermute(band[-MAXSHIFT:], "pix", up)
    after = lax.ppermute(band[:MAXSHIFT], "pix", down)
    return before, after


def register_kernel(shift_ref, band_ref, before_ref, after_ref, out_ref, padded):
    rows, width = band_ref.shape
    across = width // TILE
    tall = rows + 2 * MAXSHIFT
    for j in (0, across + 1):
        padded[j] = jnp.zeros((tall, TILE), jnp.float32)
    for j in range(across):
        lanes = pl.ds(j * TILE, TILE)
        padded[j + 1, pl.ds(0, MAXSHIFT), :] = before_ref[:, lanes].astype(jnp.float32)
        padded[j + 1, pl.ds(MAXSHIFT, rows), :] = band_ref[:, lanes].astype(jnp.float32)
        padded[j + 1, pl.ds(rows + MAXSHIFT, MAXSHIFT), :] = after_ref[:, lanes].astype(jnp.float32)

    gap = lax.broadcasted_iota(jnp.int32, (2 * TILE, TILE), 0) - lax.broadcasted_iota(
        jnp.int32, (2 * TILE, TILE), 1
    )

    @pl.loop(0, rows // TILE)
    def _(a):
        for b in range(across):
            place = (a * across + b) * 2
            dy = shift_ref[place]
            dx = shift_ref[place + 1]
            left = dx < 0
            start = jnp.where(left, b, b + 1)
            at = pl.ds(a * TILE + MAXSHIFT + dy, TILE)
            window = jnp.concatenate([padded[start, at, :], padded[start + 1, at, :]], axis=1)
            pick = (gap == jnp.where(left, dx + TILE, dx)).astype(jnp.float32).astype(jnp.bfloat16)
            moved = jnp.dot(window.astype(jnp.bfloat16), pick, preferred_element_type=jnp.float32)
            out_ref[pl.ds(pl.multiple_of(a * TILE, TILE), TILE), b * TILE : (b + 1) * TILE] = moved.astype(
                jnp.bfloat16
            )


def register(band, before, after, shifts):
    rows, width = band.shape
    vmem = pl.BlockSpec(memory_space=pltpu.VMEM)
    return pl.pallas_call(
        register_kernel,
        out_shape=jax.ShapeDtypeStruct((rows, width), jnp.bfloat16),
        in_specs=[pl.BlockSpec(memory_space=pltpu.SMEM), vmem, vmem, vmem],
        out_specs=vmem,
        scratch_shapes=[pltpu.VMEM((width // TILE + 2, rows + 2 * MAXSHIFT, TILE), jnp.float32)],
        compiler_params=pltpu.CompilerParams(vmem_limit_bytes=24 << 20),
        name="register",
    )(shifts.reshape(-1), band, before, after)


def project_step(local, x, blocks, ids, row_ref, col_ref, mix_ref):
    frames, side, cols = x.shape
    foot_cols = blocks.shape[1]
    half = row_ref.shape[0] // frames
    moved = x.reshape(frames * side, cols)
    chunk = row_ref.shape[0]
    along_rows = jnp.concatenate(
        [
            jnp.dot(row_ref[...], moved[i : i + chunk], preferred_element_type=jnp.float32)
            for i in range(0, frames * side, chunk)
        ],
        axis=0,
    ).astype(jnp.bfloat16)
    along_cols = jnp.dot(along_rows, col_ref[...], preferred_element_type=jnp.float32).astype(jnp.bfloat16)
    patches = cols // side
    low = lax.broadcasted_iota(jnp.int32, (frames, LANES), 1) < side
    pieces = [[] for _ in range(patches)]
    for h in range(side // half):
        stack = [moved[f * side + h * half : f * side + (h + 1) * half] for f in range(frames)]
        stack += [along_cols[f * side + h * half : f * side + (h + 1) * half] for f in range(frames)]
        clean = jnp.dot(mix_ref[...], jnp.concatenate(stack, axis=0), preferred_element_type=jnp.float32)
        for i in range(half // 2):
            for j in range(cols // LANES):
                first = clean[2 * i * frames : (2 * i + 1) * frames, j * LANES : (j + 1) * LANES]
                second = clean[(2 * i + 1) * frames : (2 * i + 2) * frames, j * LANES : (j + 1) * LANES]
                pieces[2 * j].append(jnp.where(low, first, pltpu.roll(second, side, 1)))
                pieces[2 * j + 1].append(jnp.where(low, pltpu.roll(first, side, 1), second))
    pixels = jnp.concatenate([jnp.concatenate(p, axis=1) for p in pieces], axis=0).astype(jnp.bfloat16)
    blocks = blocks.reshape(patches * foot_cols, side * side)
    product = lax.dot_general(pixels, blocks, (((1,), (1,)), ((), ())), preferred_element_type=jnp.float32)
    count = product.shape[1]
    owner_patch = lax.broadcasted_iota(jnp.int32, (frames, count), 1) // foot_cols
    partial = jnp.zeros((frames, count), jnp.float32)
    for p in range(patches):
        partial = jnp.where(owner_patch == p, product[p * frames : (p + 1) * frames], partial)
    owner = jnp.broadcast_to(ids // local, (frames, count))
    within = ids % local
    onehot = (
        (lax.broadcasted_iota(jnp.int32, (local, count), 0) == within).astype(jnp.float32).astype(jnp.bfloat16)
    )
    owner_order = list(range(0, NEURONS // local, 2)) + list(range(1, NEURONS // local, 2))
    total = None
    rest = partial
    for _ in range(3):
        piece = rest.astype(jnp.bfloat16).astype(jnp.float32)
        rest = rest - piece
        spread = jnp.concatenate(
            [jnp.where(owner == o, piece, 0.0) for o in owner_order], axis=0
        ).astype(jnp.bfloat16)
        term = lax.dot_general(spread, onehot, (((1,), (1,)), ((), ())), preferred_element_type=jnp.float32)
        total = term if total is None else total + term
    return total


def fused_kernel(
    local,
    shift_hbm,
    movie_ref,
    foot_ref,
    ids_hbm,
    row_hbm,
    col_hbm,
    mix_hbm,
    out_ref,
    shift_ref,
    ids_ref,
    band,
    before,
    after,
    padded,
    slabs,
    moved,
    feet,
    row_ref,
    col_ref,
    mix_ref,
    labels,
    sums,
    other,
    kept,
    landed,
    load,
    table,
    feed,
    halo_send,
    halo_recv,
    send,
    recv,
    here,
    pair_send,
    pair_recv,
    last_send,
    last_recv,
):
    groups, side, width = slabs.shape
    steps = feet.shape[0]
    wide = width // steps
    rows = band.shape[0]
    across = width // TILE
    me = lax.axis_index("tm")
    pix = lax.axis_index("pix")
    bands = lax.axis_size("pix")
    half = groups // 2
    upper = me // half
    mesh_id = pl.DeviceIdType.MESH

    barrier = pltpu.get_barrier_semaphore()
    for d in range(1, groups):
        pl.semaphore_signal(barrier, inc=1, device_id={"tm": lax.rem(me + d, groups)}, device_id_type=mesh_id)
    for d in range(1, bands):
        pl.semaphore_signal(barrier, inc=1, device_id={"pix": lax.rem(pix + d, bands)}, device_id_type=mesh_id)

    inner = TILE - MAXSHIFT
    parts = ((inner, rows - inner), (0, inner), (rows - inner, rows))

    def load_copy(i):
        first, last = parts[i]
        at = pl.ds(first, last - first)
        return pltpu.make_async_copy(movie_ref.at[at], band.at[at], load.at[i])

    table_copies = [
        pltpu.make_async_copy(src, dst, table.at[i])
        for i, (src, dst) in enumerate(
            ((row_hbm, row_ref), (col_hbm, col_ref), (mix_hbm, mix_ref), (ids_hbm, ids_ref))
        )
    ]
    shift_copy = pltpu.make_async_copy(shift_hbm, shift_ref, table.at[4])

    def feet_copy(s):
        return pltpu.make_async_copy(foot_ref.at[pl.ds(s * GROUP, GROUP)], feet.at[s], feed.at[s])

    shift_copy.start()
    for i in range(3):
        load_copy(i).start()
    for copy in table_copies:
        copy.start()

    tall = rows + 2 * MAXSHIFT
    for j in (0, across + 1):
        padded[j] = jnp.zeros((tall, TILE), jnp.float32)

    def widen(i):
        first, last = parts[i]
        for j in range(across):
            lanes = pl.ds(j * TILE, TILE)
            padded[j + 1, pl.ds(first + MAXSHIFT, last - first), :] = band[first:last, lanes].astype(jnp.float32)

    gap = lax.broadcasted_iota(jnp.int32, (2 * TILE, TILE), 0) - lax.broadcasted_iota(
        jnp.int32, (2 * TILE, TILE), 1
    )

    def register_row(a):
        for b in range(across):
            dy = shift_ref[a, 0, b]
            dx = shift_ref[a, 1, b]
            left = dx < 0
            start = jnp.where(left, b, b + 1)
            at = pl.ds(a * TILE + MAXSHIFT + dy, TILE)
            window = jnp.concatenate([padded[start, at, :], padded[start + 1, at, :]], axis=1)
            pick = (gap == jnp.where(left, dx + TILE, dx)).astype(jnp.float32).astype(jnp.bfloat16)
            tile = jnp.dot(window.astype(jnp.bfloat16), pick, preferred_element_type=jnp.float32)
            slabs[pl.ds(2 * a, 2), :, b * TILE : (b + 1) * TILE] = tile.astype(jnp.bfloat16).reshape(2, side, TILE)

    def tile_row(i):
        up = jnp.where(i == 0, 1, jnp.where(i == 1, 2, jnp.where(i == 2, 0, 3)))
        return jnp.where(upper == 1, up, 3 - up)

    def send_copy(s, to):
        lanes = pl.ds(pl.multiple_of(s * wide, wide), wide)
        return pltpu.make_async_remote_copy(
            src_ref=slabs.at[to, :, lanes],
            dst_ref=moved.at[me, :, lanes],
            send_sem=send.at[s],
            recv_sem=recv.at[s],
            device_id={"tm": to},
            device_id_type=mesh_id,
        )

    def chunk_wait(s, sem):
        lanes = pl.ds(pl.multiple_of(s * wide, wide), wide)
        taken = moved.at[pl.ds(0, groups - 1), :, lanes]
        pltpu.make_async_copy(taken, taken, sem.at[s]).wait()

    def halo_copy(i):
        source = (rows - MAXSHIFT, 0)[i]
        return pltpu.make_async_remote_copy(
            src_ref=movie_ref.at[pl.ds(source, MAXSHIFT)],
            dst_ref=(before, after)[i],
            send_sem=halo_send.at[i],
            recv_sem=halo_recv.at[i],
            device_id={"pix": (pix + 1, pix - 1)[i]},
            device_id_type=mesh_id,
        )

    sends_halo = (pix < bands - 1, pix > 0)
    gets_halo = (pix > 0, pix < bands - 1)

    load_copy(0).wait()
    widen(0)
    shift_copy.wait()
    nearest = tile_row(0)
    register_row(nearest)

    pl.semaphore_wait(barrier, groups + bands - 2)

    for i in range(2):

        @pl.when(sends_halo[i])
        def _():
            halo_copy(i).start()

    @pl.loop(0, EARLY)
    def _(s):
        for e in range(2):
            send_copy(s, 2 * nearest + e).start()

    @pl.loop(1, 4)
    def _(i):
        @pl.when(i == 2)
        def _():
            for k in (1, 2):
                load_copy(k).wait()
                widen(k)
            for k in range(2):

                @pl.when(gets_halo[k])
                def _():
                    halo_copy(k).wait_recv()

                @pl.when(jnp.logical_not(gets_halo[k]))
                def _():
                    (before, after)[k][...] = jnp.zeros((MAXSHIFT, width), jnp.bfloat16)

            for j in range(across):
                lanes = pl.ds(j * TILE, TILE)
                padded[j + 1, pl.ds(0, MAXSHIFT), :] = before[:, lanes].astype(jnp.float32)
                padded[j + 1, pl.ds(rows + MAXSHIFT, MAXSHIFT), :] = after[:, lanes].astype(jnp.float32)

        register_row(tile_row(i))

    own = pltpu.make_async_copy(slabs.at[me], moved.at[me], here)
    own.start()
    spot = lax.rem(me, half)
    targets = [(1 - upper) * half + lax.rem(spot + e, half) for e in range(half)]
    targets += [upper * half + lax.rem(spot + e, half) for e in range(1, half)]

    @pl.loop(0, steps)
    def _(s):
        for to in targets:

            @pl.when(jnp.logical_or(s >= EARLY, to // 2 != nearest))
            def _():
                send_copy(s, to).start()

    @pl.loop(0, steps)
    def _(s):
        feet_copy(s).start()

    sums[...] = jnp.zeros_like(sums)
    for copy in table_copies:
        copy.wait()
    for s in range(steps):
        labels[s] = jnp.concatenate([ids_ref[p : p + 1, :] for p in range(s * GROUP, (s + 1) * GROUP)], axis=1)
    for i in range(2):

        @pl.when(sends_halo[i])
        def _():
            halo_copy(i).wait_send()

    own.wait()

    @pl.loop(0, steps)
    def _(s):
        feet_copy(s).wait()
        chunk_wait(s, recv)
        lanes = pl.ds(pl.multiple_of(s * wide, wide), wide)
        sums[...] += project_step(local, moved[:, :, lanes], feet[s], labels[s], row_ref, col_ref, mix_ref)

    @pl.loop(0, steps)
    def _(s):
        chunk_wait(s, send)

    frames = groups
    core = lax.rem(pix, 2)
    count = groups * bands // 2
    block = count * frames
    pair_copy = pltpu.make_async_remote_copy(
        src_ref=sums.at[pl.ds(pl.multiple_of((1 - core) * block, block), block)],
        dst_ref=other,
        send_sem=pair_send,
        recv_sem=pair_recv,
        device_id={"pix": pix + 1 - 2 * core},
        device_id_type=mesh_id,
    )
    pair_copy.start()
    pair_copy.wait_recv()
    kept[...] = sums[pl.ds(pl.multiple_of(core * block, block), block), :] + other[...]
    place = me * (bands // 2) + pix // 2

    def last_copy(d):
        to = lax.rem(place + d, count)
        return pltpu.make_async_remote_copy(
            src_ref=kept.at[pl.ds(pl.multiple_of(to * frames, frames), frames)],
            dst_ref=landed.at[place],
            send_sem=last_send,
            recv_sem=last_recv,
            device_id={"tm": to // (bands // 2), "pix": lax.rem(to, bands // 2) * 2 + core},
            device_id_type=mesh_id,
        )

    for d in range(1, count):
        last_copy(d).start()
    landed[place] = kept[pl.ds(pl.multiple_of(place * frames, frames), frames), :]
    taken = landed.at[pl.ds(0, count - 1)]
    pltpu.make_async_copy(taken, taken, last_recv).wait()
    out_ref[...] = jnp.sum(landed[...], axis=0)
    pltpu.make_async_copy(taken, taken, last_send).wait()
    pair_copy.wait_send()


def fused(band, shifts, footprints, ids, groups, bands):
    rows, width = band.shape
    frames = groups
    owners = groups * bands
    steps = width // (GROUP * PATCH)
    foot_cols = footprints.shape[1]
    local = NEURONS // owners
    base = gauss_table(PATCH, pixel_sigma)
    time = gauss_table(frames, frame_sigma)
    full = GROUP * PATCH
    eye = np.eye(GROUP, dtype=np.float32)
    row_table = np.kron(eye, base.astype(np.float32)).astype(ml_dtypes.bfloat16)
    col_table = np.kron(eye, base.astype(np.float32).T).astype(ml_dtypes.bfloat16)
    half = full // frames
    spots = np.eye(half, dtype=np.float32)
    keep = np.einsum("gf,rs->rgfs", np.eye(frames, dtype=np.float32), spots)
    blur = np.einsum("gf,rs->rgfs", time.astype(np.float32), spots)
    mix = np.concatenate([keep.reshape(full, full), -blur.reshape(full, full)], axis=1).astype(ml_dtypes.bfloat16)
    hbm = pl.BlockSpec(memory_space=pltpu.HBM)
    tall = rows + 2 * MAXSHIFT
    bf16, f32, dma = jnp.bfloat16, jnp.float32, pltpu.SemaphoreType.DMA
    count = owners // 2
    return pl.pallas_call(
        lambda *refs: fused_kernel(local, *refs),
        out_shape=jax.ShapeDtypeStruct((frames, local), f32),
        in_specs=[hbm] * 7,
        out_specs=pl.BlockSpec(memory_space=pltpu.VMEM),
        scratch_shapes=[
            pltpu.SMEM(shifts.shape, jnp.int32),
            pltpu.VMEM(ids.shape, jnp.int32),
            pltpu.VMEM((rows, width), bf16),
            pltpu.VMEM((MAXSHIFT, width), bf16),
            pltpu.VMEM((MAXSHIFT, width), bf16),
            pltpu.VMEM((width // TILE + 2, tall, TILE), f32),
            pltpu.VMEM((groups, PATCH, width), bf16),
            pltpu.VMEM((groups, PATCH, width), bf16),
            pltpu.VMEM((steps, GROUP, foot_cols, PATCH * PATCH), bf16),
            pltpu.VMEM(row_table.shape, bf16),
            pltpu.VMEM(col_table.shape, bf16),
            pltpu.VMEM(mix.shape, bf16),
            pltpu.VMEM((steps, 1, GROUP * foot_cols), jnp.int32),
            pltpu.VMEM((owners * frames, local), f32),
            pltpu.VMEM((count * frames, local), f32),
            pltpu.VMEM((count * frames, local), f32),
            pltpu.VMEM((count, frames, local), f32),
            dma((3,)),
            dma((5,)),
            dma((steps,)),
            dma((2,)),
            dma((2,)),
            dma((steps,)),
            dma((steps,)),
            dma,
            dma,
            dma,
            dma,
            dma,
        ],
        compiler_params=pltpu.CompilerParams(
            vmem_limit_bytes=60 << 20, collective_id=0, has_side_effects=True
        ),
        name="fused",
    )(
        shifts,
        band,
        footprints,
        ids,
        jnp.asarray(row_table),
        jnp.asarray(col_table),
        jnp.asarray(mix),
    )


def project_general(moved, footprints, labels, owners):
    frames, side, width = moved.shape
    base = jnp.asarray(gauss_table(side, pixel_sigma))
    time = jnp.asarray(gauss_table(frames, frame_sigma))
    blocks = moved.reshape(frames, side, width // side, side)
    dot = lambda spec, a, b: jnp.einsum(spec, a, b, preferred_element_type=jnp.float32)
    along_rows = dot("ij,fjpc->fipc", base, blocks).astype(jnp.bfloat16)
    along_cols = dot("fipc,dc->fipd", along_rows, base).astype(jnp.bfloat16)
    clean = (blocks.astype(jnp.float32) - dot("gf,fipc->gipc", time, along_cols)).astype(jnp.bfloat16)
    pixels = clean.transpose(2, 0, 1, 3).reshape(width // side, frames, side * side)
    partial = dot("pfx,pkx->fpk", pixels, footprints).reshape(frames, -1)
    wanted = jnp.arange(NEURONS, dtype=jnp.int32)
    onehot = (labels.reshape(-1)[:, None] == wanted[None, :]).astype(jnp.float32)
    sums = jnp.dot(partial, onehot, precision=lax.Precision.HIGHEST, preferred_element_type=jnp.float32)
    return sums.reshape(frames, owners, -1).transpose(1, 0, 2).reshape(owners * frames, -1)


def on_device(movie, shifts, footprints, neuron_ids):
    band = movie[0]
    rows, width = band.shape
    groups = lax.axis_size("tm")
    bands = lax.axis_size("pix")
    owners = groups * bands
    wide = footprints.shape[1] * PATCH
    frames = groups * movie.shape[0]
    fits = (
        frames == groups
        and rows == 4 * TILE
        and rows == groups * PATCH
        and frames * 32 == GROUP * PATCH
        and wide == width
        and bands % 2 == 0
        and NEURONS // owners == LANES
    )
    if fits:
        return fused(band, shifts[0].transpose(0, 2, 1), footprints[0], neuron_ids[0], groups, bands).T
    before, after = halo(band)
    registered = register(band, before, after, shifts)
    slabs = registered.reshape(rows // PATCH, PATCH, width // wide, wide)
    slabs = slabs.transpose(0, 2, 1, 3).reshape(groups, PATCH, wide)
    moved = lax.all_to_all(slabs, "tm", split_axis=0, concat_axis=0, tiled=True)
    sums = project_general(moved, footprints[0], neuron_ids[0], owners)
    sums = lax.all_to_all(
        sums.reshape(owners, frames, -1), ("tm", "pix"), split_axis=0, concat_axis=0, tiled=True
    )
    return jnp.sum(sums, axis=0).T


def solution(mesh):
    in_specs = (
        P("tm", "pix", None),
        P("tm", "pix", None, None),
        P("pix", "tm", None, None),
        P("pix", "tm", None),
    )
    out_specs = P(("tm", "pix"), None)
    return jax.shard_map(
        on_device, mesh=mesh, in_specs=in_specs, out_specs=out_specs, check_vma=False
    )
```

```python
import jax
import jax.numpy as jnp
import ml_dtypes
import numpy as np
from jax import lax
from jax.experimental import pallas as pl
from jax.experimental.pallas import tpu as pltpu
from jax.sharding import PartitionSpec as P

TILE = 128
MAXSHIFT = 16
PATCH = 64
NEURONS = 4096
LANES = 128
GROUP = 4
EARLY = 2
UNIT = 4


pixel_sigma = 3.0
frame_sigma = 4.0


def gauss_table(count, sigma):
    places = np.arange(count).astype(np.float32)
    apart = places[:, None] - places[None, :]
    weights = np.exp(-apart * apart / np.float32(2.0 * sigma * sigma)).astype(np.float32)
    table = weights / np.sum(weights, axis=1, keepdims=True, dtype=np.float32)
    return table.astype(ml_dtypes.bfloat16)


def halo(band):
    count = lax.axis_size("pix")
    up = [(i, i + 1) for i in range(count - 1)]
    down = [(i + 1, i) for i in range(count - 1)]
    before = lax.ppermute(band[-MAXSHIFT:], "pix", up)
    after = lax.ppermute(band[:MAXSHIFT], "pix", down)
    return before, after


def register_kernel(shift_ref, band_ref, before_ref, after_ref, out_ref, padded):
    rows, width = band_ref.shape
    across = width // TILE
    tall = rows + 2 * MAXSHIFT
    for j in (0, across + 1):
        padded[j] = jnp.zeros((tall, TILE), jnp.float32)
    for j in range(across):
        lanes = pl.ds(j * TILE, TILE)
        padded[j + 1, pl.ds(0, MAXSHIFT), :] = before_ref[:, lanes].astype(jnp.float32)
        padded[j + 1, pl.ds(MAXSHIFT, rows), :] = band_ref[:, lanes].astype(jnp.float32)
        padded[j + 1, pl.ds(rows + MAXSHIFT, MAXSHIFT), :] = after_ref[:, lanes].astype(jnp.float32)

    gap = lax.broadcasted_iota(jnp.int32, (2 * TILE, TILE), 0) - lax.broadcasted_iota(
        jnp.int32, (2 * TILE, TILE), 1
    )

    @pl.loop(0, rows // TILE)
    def _(a):
        for b in range(across):
            place = (a * across + b) * 2
            dy = shift_ref[place]
            dx = shift_ref[place + 1]
            left = dx < 0
            start = jnp.where(left, b, b + 1)
            at = pl.ds(a * TILE + MAXSHIFT + dy, TILE)
            window = jnp.concatenate([padded[start, at, :], padded[start + 1, at, :]], axis=1)
            pick = (gap == jnp.where(left, dx + TILE, dx)).astype(jnp.float32).astype(jnp.bfloat16)
            moved = jnp.dot(window.astype(jnp.bfloat16), pick, preferred_element_type=jnp.float32)
            out_ref[pl.ds(pl.multiple_of(a * TILE, TILE), TILE), b * TILE : (b + 1) * TILE] = moved.astype(
                jnp.bfloat16
            )


def register(band, before, after, shifts):
    rows, width = band.shape
    vmem = pl.BlockSpec(memory_space=pltpu.VMEM)
    return pl.pallas_call(
        register_kernel,
        out_shape=jax.ShapeDtypeStruct((rows, width), jnp.bfloat16),
        in_specs=[pl.BlockSpec(memory_space=pltpu.SMEM), vmem, vmem, vmem],
        out_specs=vmem,
        scratch_shapes=[pltpu.VMEM((width // TILE + 2, rows + 2 * MAXSHIFT, TILE), jnp.float32)],
        compiler_params=pltpu.CompilerParams(vmem_limit_bytes=24 << 20),
        name="register",
    )(shifts.reshape(-1), band, before, after)


def project_step(local, x, blocks, ids, row_ref, col_ref, mix_ref):
    frames, side, cols = x.shape
    foot_cols = blocks.shape[1]
    half = row_ref.shape[0] // frames
    moved = x.reshape(frames * side, cols)
    chunk = row_ref.shape[0]
    along_rows = jnp.concatenate(
        [
            jnp.dot(row_ref[...], moved[i : i + chunk], preferred_element_type=jnp.float32)
            for i in range(0, frames * side, chunk)
        ],
        axis=0,
    ).astype(jnp.bfloat16)
    along_cols = jnp.dot(along_rows, col_ref[...], preferred_element_type=jnp.float32).astype(jnp.bfloat16)
    patches = cols // side
    low = lax.broadcasted_iota(jnp.int32, (frames, LANES), 1) < side
    pieces = [[] for _ in range(patches)]
    for h in range(side // half):
        stack = [moved[f * side + h * half : f * side + (h + 1) * half] for f in range(frames)]
        stack += [along_cols[f * side + h * half : f * side + (h + 1) * half] for f in range(frames)]
        clean = jnp.dot(mix_ref[...], jnp.concatenate(stack, axis=0), preferred_element_type=jnp.float32)
        for i in range(half // 2):
            for j in range(cols // LANES):
                first = clean[2 * i * frames : (2 * i + 1) * frames, j * LANES : (j + 1) * LANES]
                second = clean[(2 * i + 1) * frames : (2 * i + 2) * frames, j * LANES : (j + 1) * LANES]
                pieces[2 * j].append(jnp.where(low, first, pltpu.roll(second, side, 1)))
                pieces[2 * j + 1].append(jnp.where(low, pltpu.roll(first, side, 1), second))
    pixels = jnp.concatenate([jnp.concatenate(p, axis=1) for p in pieces], axis=0).astype(jnp.bfloat16)
    blocks = blocks.reshape(patches * foot_cols, side * side)
    product = lax.dot_general(pixels, blocks, (((1,), (1,)), ((), ())), preferred_element_type=jnp.float32)
    count = product.shape[1]
    owner_patch = lax.broadcasted_iota(jnp.int32, (frames, count), 1) // foot_cols
    partial = jnp.zeros((frames, count), jnp.float32)
    for p in range(patches):
        partial = jnp.where(owner_patch == p, product[p * frames : (p + 1) * frames], partial)
    owner = jnp.broadcast_to(ids // local, (frames, count))
    within = ids % local
    onehot = (
        (lax.broadcasted_iota(jnp.int32, (local, count), 0) == within).astype(jnp.float32).astype(jnp.bfloat16)
    )
    owner_order = list(range(0, NEURONS // local, 2)) + list(range(1, NEURONS // local, 2))
    total = None
    rest = partial
    for _ in range(3):
        piece = rest.astype(jnp.bfloat16).astype(jnp.float32)
        rest = rest - piece
        spread = jnp.concatenate(
            [jnp.where(owner == o, piece, 0.0) for o in owner_order], axis=0
        ).astype(jnp.bfloat16)
        term = lax.dot_general(spread, onehot, (((1,), (1,)), ((), ())), preferred_element_type=jnp.float32)
        total = term if total is None else total + term
    return total


def fused_kernel(
    local,
    shift_hbm,
    movie_ref,
    foot_ref,
    ids_hbm,
    row_hbm,
    col_hbm,
    mix_hbm,
    out_ref,
    shift_ref,
    ids_ref,
    band,
    before,
    after,
    padded,
    slabs,
    moved,
    feet,
    row_ref,
    col_ref,
    mix_ref,
    labels,
    sums,
    other,
    kept,
    landed,
    load,
    table,
    feed,
    halo_send,
    halo_recv,
    send,
    recv,
    here,
    pair_send,
    pair_recv,
    last_send,
    last_recv,
    ready,
):
    groups, side, width = slabs.shape
    steps = feet.shape[0]
    wide = width // steps
    rows = band.shape[0]
    across = width // TILE
    me = lax.axis_index("tm")
    pix = lax.axis_index("pix")
    bands = lax.axis_size("pix")
    half = groups // 2
    upper = me // half
    mesh_id = pl.DeviceIdType.MESH

    per = TILE // side
    last = groups // per - 1
    quarter = me // per
    inside = jnp.logical_and(quarter > 0, quarter < last)

    barrier = pltpu.get_barrier_semaphore()

    def greet(**place):
        pl.semaphore_signal(barrier, inc=1, device_id=place, device_id_type=mesh_id)

    @pl.when(inside)
    def _():
        for e in range(per):
            greet(tm=(last - quarter) * per + e)

    for d in range(1, bands):
        greet(pix=lax.rem(pix + d, bands))
    for t in [*range(per), *range(last * per, groups)]:

        @pl.when(me != t)
        def _():
            greet(tm=t)

    reach = TILE + 2 * MAXSHIFT
    first = jnp.where(upper == 1, TILE - MAXSHIFT, 2 * TILE - MAXSHIFT)
    second = jnp.where(upper == 1, 2 * TILE + MAXSHIFT, TILE - MAXSHIFT)
    ends = TILE - MAXSHIFT
    parts = ((first, reach), (second, TILE), (0, ends), (rows - ends, ends))

    def load_copy(i):
        at = pl.ds(pl.multiple_of(parts[i][0], MAXSHIFT), parts[i][1])
        return pltpu.make_async_copy(movie_ref.at[at], band.at[at], load.at[i])

    table_copies = [
        pltpu.make_async_copy(src, dst, table.at[i])
        for i, (src, dst) in enumerate(
            ((row_hbm, row_ref), (col_hbm, col_ref), (mix_hbm, mix_ref), (ids_hbm, ids_ref))
        )
    ]
    shift_copy = pltpu.make_async_copy(shift_hbm, shift_ref, table.at[4])

    def feet_copy(s):
        return pltpu.make_async_copy(foot_ref.at[pl.ds(s * GROUP, GROUP)], feet.at[s], feed.at[s])

    shift_copy.start()
    for i in range(4):
        load_copy(i).start()
    for copy in table_copies:
        copy.start()

    tall = rows + 2 * MAXSHIFT
    for j in (0, across + 1):
        padded[j] = jnp.zeros((tall, TILE), jnp.float32)

    def widen(i):
        load_copy(i).wait()
        place = pl.multiple_of(parts[i][0], MAXSHIFT)
        for j in range(across):
            lanes = pl.ds(j * TILE, TILE)
            part = band[pl.ds(place, parts[i][1]), lanes]
            padded[j + 1, pl.ds(place + MAXSHIFT, parts[i][1]), :] = part.astype(jnp.float32)

    gap = lax.broadcasted_iota(jnp.int32, (2 * TILE, TILE), 0) - lax.broadcasted_iota(
        jnp.int32, (2 * TILE, TILE), 1
    )

    def register_tiles(a, g):
        for e in range(UNIT):
            b = g * UNIT + e
            dy = shift_ref[a, 0, b]
            dx = shift_ref[a, 1, b]
            left = dx < 0
            start = jnp.where(left, b, b + 1)
            at = pl.ds(a * TILE + MAXSHIFT + dy, TILE)
            window = jnp.concatenate([padded[start, at, :], padded[start + 1, at, :]], axis=1)
            pick = (gap == jnp.where(left, dx + TILE, dx)).astype(jnp.float32).astype(jnp.bfloat16)
            tile = jnp.dot(window.astype(jnp.bfloat16), pick, preferred_element_type=jnp.float32)
            lanes = pl.ds(pl.multiple_of(b * TILE, TILE), TILE)
            slabs[pl.ds(per * a, per), :, lanes] = tile.astype(jnp.bfloat16).reshape(per, side, TILE)

    def tile_row(i):
        up = jnp.where(i == 0, 1, jnp.where(i == 1, 2, jnp.where(i == 2, 0, 3)))
        return jnp.where(upper == 1, up, 3 - up)

    def send_copy(s, to):
        lanes = pl.ds(pl.multiple_of(s * wide, wide), wide)
        return pltpu.make_async_remote_copy(
            src_ref=slabs.at[to, :, lanes],
            dst_ref=moved.at[me, :, lanes],
            send_sem=send.at[s],
            recv_sem=recv.at[s],
            device_id={"tm": to},
            device_id_type=mesh_id,
        )

    def chunk_wait(s, sem):
        lanes = pl.ds(pl.multiple_of(s * wide, wide), wide)
        taken = moved.at[pl.ds(0, groups - 1), :, lanes]
        pltpu.make_async_copy(taken, taken, sem.at[s]).wait()

    def halo_copy(i):
        source = (rows - MAXSHIFT, 0)[i]
        return pltpu.make_async_remote_copy(
            src_ref=movie_ref.at[pl.ds(source, MAXSHIFT)],
            dst_ref=(before, after)[i],
            send_sem=halo_send.at[i],
            recv_sem=halo_recv.at[i],
            device_id={"pix": (pix + 1, pix - 1)[i]},
            device_id_type=mesh_id,
        )

    sends_halo = (pix < bands - 1, pix > 0)
    gets_halo = (pix > 0, pix < bands - 1)

    units = across // UNIT
    nearest = tile_row(0)
    enter = jnp.where(quarter == 0, 2 * units, EARLY * wide // (UNIT * TILE))
    widen(0)
    shift_copy.wait()

    @pl.loop(0, 4 * units)
    def _(u):
        @pl.when(u == enter)
        def _():
            pl.semaphore_wait(barrier, jnp.where(inside, per, groups - 1) + bands - 1)
            for i in range(2):

                @pl.when(sends_halo[i])
                def _():
                    halo_copy(i).start()

            @pl.loop(0, EARLY)
            def _(s):
                for e in range(per):
                    send_copy(s, per * nearest + e).start()

            @pl.when(quarter == last)
            def _():
                for q in range(1, last):
                    to = {"tm": q * per + lax.rem(me, per)}
                    pl.semaphore_signal(ready, inc=1, device_id=to, device_id_type=mesh_id)

        @pl.when(u == units)
        def _():
            widen(1)

        @pl.when(u == 2 * units)
        def _():
            widen(2)
            widen(3)
            for k in range(2):

                @pl.when(gets_halo[k])
                def _():
                    halo_copy(k).wait_recv()

                @pl.when(jnp.logical_not(gets_halo[k]))
                def _():
                    (before, after)[k][...] = jnp.zeros((MAXSHIFT, width), jnp.bfloat16)

            for j in range(across):
                lanes = pl.ds(j * TILE, TILE)
                padded[j + 1, pl.ds(0, MAXSHIFT), :] = before[:, lanes].astype(jnp.float32)
                padded[j + 1, pl.ds(rows + MAXSHIFT, MAXSHIFT), :] = after[:, lanes].astype(jnp.float32)

        register_tiles(tile_row(u // units), lax.rem(u, units))

    @pl.when(inside)
    def _():
        pl.semaphore_wait(ready, 1)

    own = pltpu.make_async_copy(slabs.at[me], moved.at[me], here)
    own.start()
    spot = lax.rem(me, half)
    targets = [(1 - upper) * half + lax.rem(spot + e, half) for e in range(half)]
    targets += [upper * half + lax.rem(spot + e, half) for e in range(1, half)]

    @pl.loop(0, steps)
    def _(s):
        for to in targets:

            @pl.when(jnp.logical_or(s >= EARLY, to // per != nearest))
            def _():
                send_copy(s, to).start()

    @pl.loop(0, steps)
    def _(s):
        feet_copy(s).start()

    sums[...] = jnp.zeros_like(sums)
    for copy in table_copies:
        copy.wait()
    for s in range(steps):
        labels[s] = jnp.concatenate([ids_ref[p : p + 1, :] for p in range(s * GROUP, (s + 1) * GROUP)], axis=1)
    for i in range(2):

        @pl.when(sends_halo[i])
        def _():
            halo_copy(i).wait_send()

    own.wait()

    @pl.loop(0, steps)
    def _(s):
        feet_copy(s).wait()
        chunk_wait(s, recv)
        lanes = pl.ds(pl.multiple_of(s * wide, wide), wide)
        sums[...] += project_step(local, moved[:, :, lanes], feet[s], labels[s], row_ref, col_ref, mix_ref)

    @pl.loop(0, steps)
    def _(s):
        chunk_wait(s, send)

    frames = groups
    core = lax.rem(pix, 2)
    count = groups * bands // 2
    block = count * frames
    pair_copy = pltpu.make_async_remote_copy(
        src_ref=sums.at[pl.ds(pl.multiple_of((1 - core) * block, block), block)],
        dst_ref=other,
        send_sem=pair_send,
        recv_sem=pair_recv,
        device_id={"pix": pix + 1 - 2 * core},
        device_id_type=mesh_id,
    )
    pair_copy.start()
    pair_copy.wait_recv()
    kept[...] = sums[pl.ds(pl.multiple_of(core * block, block), block), :] + other[...]
    place = me * (bands // 2) + pix // 2

    def last_copy(d):
        to = lax.rem(place + d, count)
        return pltpu.make_async_remote_copy(
            src_ref=kept.at[pl.ds(pl.multiple_of(to * frames, frames), frames)],
            dst_ref=landed.at[place],
            send_sem=last_send,
            recv_sem=last_recv,
            device_id={"tm": to // (bands // 2), "pix": lax.rem(to, bands // 2) * 2 + core},
            device_id_type=mesh_id,
        )

    for d in range(1, count):
        last_copy(d).start()
    landed[place] = kept[pl.ds(pl.multiple_of(place * frames, frames), frames), :]
    taken = landed.at[pl.ds(0, count - 1)]
    pltpu.make_async_copy(taken, taken, last_recv).wait()
    out_ref[...] = jnp.sum(landed[...], axis=0)
    pltpu.make_async_copy(taken, taken, last_send).wait()
    pair_copy.wait_send()


def fused(band, shifts, footprints, ids, groups, bands):
    rows, width = band.shape
    frames = groups
    owners = groups * bands
    steps = width // (GROUP * PATCH)
    foot_cols = footprints.shape[1]
    local = NEURONS // owners
    base = gauss_table(PATCH, pixel_sigma)
    time = gauss_table(frames, frame_sigma)
    full = GROUP * PATCH
    eye = np.eye(GROUP, dtype=np.float32)
    row_table = np.kron(eye, base.astype(np.float32)).astype(ml_dtypes.bfloat16)
    col_table = np.kron(eye, base.astype(np.float32).T).astype(ml_dtypes.bfloat16)
    half = full // frames
    spots = np.eye(half, dtype=np.float32)
    keep = np.einsum("gf,rs->rgfs", np.eye(frames, dtype=np.float32), spots)
    blur = np.einsum("gf,rs->rgfs", time.astype(np.float32), spots)
    mix = np.concatenate([keep.reshape(full, full), -blur.reshape(full, full)], axis=1).astype(ml_dtypes.bfloat16)
    hbm = pl.BlockSpec(memory_space=pltpu.HBM)
    tall = rows + 2 * MAXSHIFT
    bf16, f32, dma = jnp.bfloat16, jnp.float32, pltpu.SemaphoreType.DMA
    count = owners // 2
    return pl.pallas_call(
        lambda *refs: fused_kernel(local, *refs),
        out_shape=jax.ShapeDtypeStruct((frames, local), f32),
        in_specs=[hbm] * 7,
        out_specs=pl.BlockSpec(memory_space=pltpu.VMEM),
        scratch_shapes=[
            pltpu.SMEM(shifts.shape, jnp.int32),
            pltpu.VMEM(ids.shape, jnp.int32),
            pltpu.VMEM((rows, width), bf16),
            pltpu.VMEM((MAXSHIFT, width), bf16),
            pltpu.VMEM((MAXSHIFT, width), bf16),
            pltpu.VMEM((width // TILE + 2, tall, TILE), f32),
            pltpu.VMEM((groups, PATCH, width), bf16),
            pltpu.VMEM((groups, PATCH, width), bf16),
            pltpu.VMEM((steps, GROUP, foot_cols, PATCH * PATCH), bf16),
            pltpu.VMEM(row_table.shape, bf16),
            pltpu.VMEM(col_table.shape, bf16),
            pltpu.VMEM(mix.shape, bf16),
            pltpu.VMEM((steps, 1, GROUP * foot_cols), jnp.int32),
            pltpu.VMEM((owners * frames, local), f32),
            pltpu.VMEM((count * frames, local), f32),
            pltpu.VMEM((count * frames, local), f32),
            pltpu.VMEM((count, frames, local), f32),
            dma((4,)),
            dma((5,)),
            dma((steps,)),
            dma((2,)),
            dma((2,)),
            dma((steps,)),
            dma((steps,)),
            dma,
            dma,
            dma,
            dma,
            dma,
            pltpu.SemaphoreType.REGULAR,
        ],
        compiler_params=pltpu.CompilerParams(
            vmem_limit_bytes=48 << 20, collective_id=0, has_side_effects=True
        ),
        name="fused",
    )(
        *(
            pltpu.with_memory_space_constraint(operand, pltpu.HBM)
            for operand in (
                shifts,
                band,
                footprints,
                ids,
                jnp.asarray(row_table),
                jnp.asarray(col_table),
                jnp.asarray(mix),
            )
        )
    )


def project_general(moved, footprints, labels, owners):
    frames, side, width = moved.shape
    base = jnp.asarray(gauss_table(side, pixel_sigma))
    time = jnp.asarray(gauss_table(frames, frame_sigma))
    blocks = moved.reshape(frames, side, width // side, side)
    dot = lambda spec, a, b: jnp.einsum(spec, a, b, preferred_element_type=jnp.float32)
    along_rows = dot("ij,fjpc->fipc", base, blocks).astype(jnp.bfloat16)
    along_cols = dot("fipc,dc->fipd", along_rows, base).astype(jnp.bfloat16)
    clean = (blocks.astype(jnp.float32) - dot("gf,fipc->gipc", time, along_cols)).astype(jnp.bfloat16)
    pixels = clean.transpose(2, 0, 1, 3).reshape(width // side, frames, side * side)
    partial = dot("pfx,pkx->fpk", pixels, footprints).reshape(frames, -1)
    wanted = jnp.arange(NEURONS, dtype=jnp.int32)
    onehot = (labels.reshape(-1)[:, None] == wanted[None, :]).astype(jnp.float32)
    sums = jnp.dot(partial, onehot, precision=lax.Precision.HIGHEST, preferred_element_type=jnp.float32)
    return sums.reshape(frames, owners, -1).transpose(1, 0, 2).reshape(owners * frames, -1)


def on_device(movie, shifts, footprints, neuron_ids):
    band = movie[0]
    rows, width = band.shape
    groups = lax.axis_size("tm")
    bands = lax.axis_size("pix")
    owners = groups * bands
    wide = footprints.shape[1] * PATCH
    frames = groups * movie.shape[0]
    fits = (
        frames == groups
        and rows == 4 * TILE
        and rows == groups * PATCH
        and frames * 32 == GROUP * PATCH
        and wide == width
        and bands % 2 == 0
        and NEURONS // owners == LANES
    )
    if fits:
        return fused(band, shifts[0].transpose(0, 2, 1), footprints[0], neuron_ids[0], groups, bands).T
    before, after = halo(band)
    registered = register(band, before, after, shifts)
    slabs = registered.reshape(rows // PATCH, PATCH, width // wide, wide)
    slabs = slabs.transpose(0, 2, 1, 3).reshape(groups, PATCH, wide)
    moved = lax.all_to_all(slabs, "tm", split_axis=0, concat_axis=0, tiled=True)
    sums = project_general(moved, footprints[0], neuron_ids[0], owners)
    sums = lax.all_to_all(
        sums.reshape(owners, frames, -1), ("tm", "pix"), split_axis=0, concat_axis=0, tiled=True
    )
    return jnp.sum(sums, axis=0).T


def solution(mesh):
    in_specs = (
        P("tm", "pix", None),
        P("tm", "pix", None, None),
        P("pix", "tm", None, None),
        P("pix", "tm", None),
    )
    out_specs = P(("tm", "pix"), None)
    return jax.shard_map(
        on_device, mesh=mesh, in_specs=in_specs, out_specs=out_specs, check_vma=False
    )
```

```python
import jax
import jax.numpy as jnp
import ml_dtypes
import numpy as np
from jax import lax
from jax.experimental import pallas as pl
from jax.experimental.pallas import tpu as pltpu
from jax.sharding import PartitionSpec as P

TILE = 128
MAXSHIFT = 16
PATCH = 64
NEURONS = 4096
LANES = 128
GROUP = 4
EARLY = 2
AHEAD = 2
UNIT = 4


pixel_sigma = 3.0
frame_sigma = 4.0


def gauss_table(count, sigma):
    places = np.arange(count).astype(np.float32)
    apart = places[:, None] - places[None, :]
    weights = np.exp(-apart * apart / np.float32(2.0 * sigma * sigma)).astype(np.float32)
    table = weights / np.sum(weights, axis=1, keepdims=True, dtype=np.float32)
    return table.astype(ml_dtypes.bfloat16)


def halo(band):
    count = lax.axis_size("pix")
    up = [(i, i + 1) for i in range(count - 1)]
    down = [(i + 1, i) for i in range(count - 1)]
    before = lax.ppermute(band[-MAXSHIFT:], "pix", up)
    after = lax.ppermute(band[:MAXSHIFT], "pix", down)
    return before, after


def register_kernel(shift_ref, band_ref, before_ref, after_ref, out_ref, padded):
    rows, width = band_ref.shape
    across = width // TILE
    tall = rows + 2 * MAXSHIFT
    for j in (0, across + 1):
        padded[j] = jnp.zeros((tall, TILE), jnp.float32)
    for j in range(across):
        lanes = pl.ds(j * TILE, TILE)
        padded[j + 1, pl.ds(0, MAXSHIFT), :] = before_ref[:, lanes].astype(jnp.float32)
        padded[j + 1, pl.ds(MAXSHIFT, rows), :] = band_ref[:, lanes].astype(jnp.float32)
        padded[j + 1, pl.ds(rows + MAXSHIFT, MAXSHIFT), :] = after_ref[:, lanes].astype(jnp.float32)

    gap = lax.broadcasted_iota(jnp.int32, (2 * TILE, TILE), 0) - lax.broadcasted_iota(
        jnp.int32, (2 * TILE, TILE), 1
    )

    @pl.loop(0, rows // TILE)
    def _(a):
        for b in range(across):
            place = (a * across + b) * 2
            dy = shift_ref[place]
            dx = shift_ref[place + 1]
            left = dx < 0
            start = jnp.where(left, b, b + 1)
            at = pl.ds(a * TILE + MAXSHIFT + dy, TILE)
            window = jnp.concatenate([padded[start, at, :], padded[start + 1, at, :]], axis=1)
            pick = (gap == jnp.where(left, dx + TILE, dx)).astype(jnp.float32).astype(jnp.bfloat16)
            moved = jnp.dot(window.astype(jnp.bfloat16), pick, preferred_element_type=jnp.float32)
            out_ref[pl.ds(pl.multiple_of(a * TILE, TILE), TILE), b * TILE : (b + 1) * TILE] = moved.astype(
                jnp.bfloat16
            )


def register(band, before, after, shifts):
    rows, width = band.shape
    vmem = pl.BlockSpec(memory_space=pltpu.VMEM)
    return pl.pallas_call(
        register_kernel,
        out_shape=jax.ShapeDtypeStruct((rows, width), jnp.bfloat16),
        in_specs=[pl.BlockSpec(memory_space=pltpu.SMEM), vmem, vmem, vmem],
        out_specs=vmem,
        scratch_shapes=[pltpu.VMEM((width // TILE + 2, rows + 2 * MAXSHIFT, TILE), jnp.float32)],
        compiler_params=pltpu.CompilerParams(vmem_limit_bytes=24 << 20),
        name="register",
    )(shifts.reshape(-1), band, before, after)


def project_step(local, x, blocks, ids, row_ref, col_ref, mix_ref):
    frames, side, cols = x.shape
    foot_cols = blocks.shape[1]
    half = row_ref.shape[0] // frames
    moved = x.reshape(frames * side, cols)
    chunk = row_ref.shape[0]
    along_rows = jnp.concatenate(
        [
            jnp.dot(row_ref[...], moved[i : i + chunk], preferred_element_type=jnp.float32)
            for i in range(0, frames * side, chunk)
        ],
        axis=0,
    ).astype(jnp.bfloat16)
    along_cols = jnp.dot(along_rows, col_ref[...], preferred_element_type=jnp.float32).astype(jnp.bfloat16)
    patches = cols // side
    low = lax.broadcasted_iota(jnp.int32, (frames, LANES), 1) < side
    pieces = [[] for _ in range(patches)]
    for h in range(side // half):
        stack = [moved[f * side + h * half : f * side + (h + 1) * half] for f in range(frames)]
        stack += [along_cols[f * side + h * half : f * side + (h + 1) * half] for f in range(frames)]
        clean = jnp.dot(mix_ref[...], jnp.concatenate(stack, axis=0), preferred_element_type=jnp.float32)
        for i in range(half // 2):
            for j in range(cols // LANES):
                first = clean[2 * i * frames : (2 * i + 1) * frames, j * LANES : (j + 1) * LANES]
                second = clean[(2 * i + 1) * frames : (2 * i + 2) * frames, j * LANES : (j + 1) * LANES]
                pieces[2 * j].append(jnp.where(low, first, pltpu.roll(second, side, 1)))
                pieces[2 * j + 1].append(jnp.where(low, pltpu.roll(first, side, 1), second))
    pixels = jnp.concatenate([jnp.concatenate(p, axis=1) for p in pieces], axis=0).astype(jnp.bfloat16)
    blocks = blocks.reshape(patches * foot_cols, side * side)
    product = lax.dot_general(pixels, blocks, (((1,), (1,)), ((), ())), preferred_element_type=jnp.float32)
    count = product.shape[1]
    owner_patch = lax.broadcasted_iota(jnp.int32, (frames, count), 1) // foot_cols
    partial = jnp.zeros((frames, count), jnp.float32)
    for p in range(patches):
        partial = jnp.where(owner_patch == p, product[p * frames : (p + 1) * frames], partial)
    owner = jnp.broadcast_to(ids // local, (frames, count))
    within = ids % local
    onehot = (
        (lax.broadcasted_iota(jnp.int32, (local, count), 0) == within).astype(jnp.float32).astype(jnp.bfloat16)
    )
    owner_order = range(NEURONS // local)
    total = None
    rest = partial
    for _ in range(3):
        piece = rest.astype(jnp.bfloat16).astype(jnp.float32)
        rest = rest - piece
        spread = jnp.concatenate(
            [jnp.where(owner == o, piece, 0.0) for o in owner_order], axis=0
        ).astype(jnp.bfloat16)
        term = lax.dot_general(spread, onehot, (((1,), (1,)), ((), ())), preferred_element_type=jnp.float32)
        total = term if total is None else total + term
    return total


def fused_kernel(
    local,
    shift_hbm,
    movie_ref,
    foot_ref,
    ids_hbm,
    row_hbm,
    col_hbm,
    mix_hbm,
    out_ref,
    shift_ref,
    ids_ref,
    band,
    before,
    after,
    padded,
    slabs,
    moved,
    feet,
    row_ref,
    col_ref,
    mix_ref,
    labels,
    sums,
    other,
    kept,
    landed,
    load,
    table,
    feed,
    halo_send,
    halo_recv,
    send,
    recv,
    here,
    pair_send,
    pair_recv,
    last_send,
    last_recv,
    ready,
):
    groups, side, width = slabs.shape
    steps = feet.shape[0]
    wide = width // steps
    rows = band.shape[0]
    across = width // TILE
    me = lax.axis_index("tm")
    pix = lax.axis_index("pix")
    bands = lax.axis_size("pix")
    half = groups // 2
    upper = me // half
    mesh_id = pl.DeviceIdType.MESH

    per = TILE // side
    last = groups // per - 1
    quarter = me // per
    inside = jnp.logical_and(quarter > 0, quarter < last)

    barrier = pltpu.get_barrier_semaphore()

    def greet(**place):
        pl.semaphore_signal(barrier, inc=1, device_id=place, device_id_type=mesh_id)

    @pl.when(inside)
    def _():
        for e in range(per):
            greet(tm=(last - quarter) * per + e)

    for d in range(1, bands):
        greet(pix=lax.rem(pix + d, bands))
    for t in [*range(per), *range(last * per, groups)]:

        @pl.when(me != t)
        def _():
            greet(tm=t)

    reach = TILE + 2 * MAXSHIFT
    first = jnp.where(upper == 1, TILE - MAXSHIFT, 2 * TILE - MAXSHIFT)
    second = jnp.where(upper == 1, 2 * TILE + MAXSHIFT, TILE - MAXSHIFT)
    ends = TILE - MAXSHIFT
    parts = ((first, reach), (second, TILE), (0, ends), (rows - ends, ends))

    def load_copy(i):
        at = pl.ds(pl.multiple_of(parts[i][0], MAXSHIFT), parts[i][1])
        return pltpu.make_async_copy(movie_ref.at[at], band.at[at], load.at[i])

    table_copies = [
        pltpu.make_async_copy(src, dst, table.at[i])
        for i, (src, dst) in enumerate(
            ((row_hbm, row_ref), (col_hbm, col_ref), (mix_hbm, mix_ref), (ids_hbm, ids_ref))
        )
    ]
    shift_copy = pltpu.make_async_copy(shift_hbm, shift_ref, table.at[4])

    def feet_copy(s):
        return pltpu.make_async_copy(foot_ref.at[pl.ds(s * GROUP, GROUP)], feet.at[s], feed.at[s])

    shift_copy.start()
    for i in range(4):
        load_copy(i).start()
    for copy in table_copies:
        copy.start()

    tall = rows + 2 * MAXSHIFT
    for j in (0, across + 1):
        padded[j] = jnp.zeros((tall, TILE), jnp.float32)

    def widen(i):
        load_copy(i).wait()
        place = pl.multiple_of(parts[i][0], MAXSHIFT)
        for j in range(across):
            lanes = pl.ds(j * TILE, TILE)
            part = band[pl.ds(place, parts[i][1]), lanes]
            padded[j + 1, pl.ds(place + MAXSHIFT, parts[i][1]), :] = part.astype(jnp.float32)

    gap = lax.broadcasted_iota(jnp.int32, (2 * TILE, TILE), 0) - lax.broadcasted_iota(
        jnp.int32, (2 * TILE, TILE), 1
    )

    def register_tiles(a, g):
        for e in range(UNIT):
            b = g * UNIT + e
            dy = shift_ref[a, 0, b]
            dx = shift_ref[a, 1, b]
            left = dx < 0
            start = jnp.where(left, b, b + 1)
            at = pl.ds(a * TILE + MAXSHIFT + dy, TILE)
            window = jnp.concatenate([padded[start, at, :], padded[start + 1, at, :]], axis=1)
            pick = (gap == jnp.where(left, dx + TILE, dx)).astype(jnp.float32).astype(jnp.bfloat16)
            tile = jnp.dot(window.astype(jnp.bfloat16), pick, preferred_element_type=jnp.float32)
            lanes = pl.ds(pl.multiple_of(b * TILE, TILE), TILE)
            slabs[pl.ds(per * a, per), :, lanes] = tile.astype(jnp.bfloat16).reshape(per, side, TILE)

    def tile_row(i):
        up = jnp.where(i == 0, 1, jnp.where(i == 1, 2, jnp.where(i == 2, 0, 3)))
        return jnp.where(upper == 1, up, 3 - up)

    def send_copy(s, to):
        lanes = pl.ds(pl.multiple_of(s * wide, wide), wide)
        return pltpu.make_async_remote_copy(
            src_ref=slabs.at[to, :, lanes],
            dst_ref=moved.at[me, :, lanes],
            send_sem=send.at[s],
            recv_sem=recv.at[s],
            device_id={"tm": to},
            device_id_type=mesh_id,
        )

    def chunk_wait(s, sem):
        lanes = pl.ds(pl.multiple_of(s * wide, wide), wide)
        taken = moved.at[pl.ds(0, groups - 1), :, lanes]
        pltpu.make_async_copy(taken, taken, sem.at[s]).wait()

    def halo_copy(i):
        source = (rows - MAXSHIFT, 0)[i]
        return pltpu.make_async_remote_copy(
            src_ref=movie_ref.at[pl.ds(source, MAXSHIFT)],
            dst_ref=(before, after)[i],
            send_sem=halo_send.at[i],
            recv_sem=halo_recv.at[i],
            device_id={"pix": (pix + 1, pix - 1)[i]},
            device_id_type=mesh_id,
        )

    sends_halo = (pix < bands - 1, pix > 0)
    gets_halo = (pix > 0, pix < bands - 1)

    units = across // UNIT
    nearest = tile_row(0)
    enter = jnp.where(quarter == 0, 2 * units, EARLY * wide // (UNIT * TILE))
    widen(0)
    shift_copy.wait()

    @pl.loop(0, 4 * units)
    def _(u):
        @pl.when(u == enter)
        def _():
            pl.semaphore_wait(barrier, jnp.where(inside, per, groups - 1) + bands - 1)
            for i in range(2):

                @pl.when(sends_halo[i])
                def _():
                    halo_copy(i).start()

            @pl.loop(0, EARLY)
            def _(s):
                for e in range(per):
                    send_copy(s, per * nearest + e).start()

            @pl.when(quarter == last)
            def _():
                for q in range(1, last):
                    to = {"tm": q * per + lax.rem(me, per)}
                    pl.semaphore_signal(ready, inc=1, device_id=to, device_id_type=mesh_id)

        @pl.when(u == units)
        def _():
            widen(1)

        @pl.when(u == 2 * units)
        def _():
            widen(2)
            widen(3)
            for k in range(2):

                @pl.when(gets_halo[k])
                def _():
                    halo_copy(k).wait_recv()

                @pl.when(jnp.logical_not(gets_halo[k]))
                def _():
                    (before, after)[k][...] = jnp.zeros((MAXSHIFT, width), jnp.bfloat16)

            for j in range(across):
                lanes = pl.ds(j * TILE, TILE)
                padded[j + 1, pl.ds(0, MAXSHIFT), :] = before[:, lanes].astype(jnp.float32)
                padded[j + 1, pl.ds(rows + MAXSHIFT, MAXSHIFT), :] = after[:, lanes].astype(jnp.float32)

        register_tiles(tile_row(u // units), lax.rem(u, units))

    @pl.when(inside)
    def _():
        pl.semaphore_wait(ready, 1)

    own = pltpu.make_async_copy(slabs.at[me], moved.at[me], here)
    own.start()
    side_x = lax.rem(me, per)
    mine = (side_x, per - 1 - side_x)
    across_z = {"o": (1 - upper) * last, "i": (1 - upper) + upper * (last // 2)}
    across_z["i"] = 2 - upper
    across_z["o"] = (1 - upper) * last
    inner_z = 1 + upper
    zz = jnp.where(inside, 1, 0)
    across_z["s"] = jnp.where(inside, across_z["i"], across_z["o"])
    across_z["d"] = jnp.where(inside, across_z["o"], across_z["i"])
    other_z = jnp.where(inside, upper * last, inner_z)
    targets = [across_z["o"] * per + mine[1], across_z["i"] * per + mine[1], across_z["o"] * per + mine[0], across_z["i"] * per + mine[0]] + [other_z * per + mine[1], quarter * per + mine[1], other_z * per + mine[0]]

    @pl.loop(0, AHEAD)
    def _(s):
        for to in targets:

            @pl.when(jnp.logical_or(s >= EARLY, to // per != nearest))
            def _():
                send_copy(s, to).start()

    @pl.loop(0, steps)
    def _(s):
        feet_copy(s).start()

    sums[...] = jnp.zeros_like(sums)
    for copy in table_copies:
        copy.wait()
    for s in range(steps):
        labels[s] = jnp.concatenate([ids_ref[p : p + 1, :] for p in range(s * GROUP, (s + 1) * GROUP)], axis=1)
    for i in range(2):

        @pl.when(sends_halo[i])
        def _():
            halo_copy(i).wait_send()

    own.wait()

    @pl.loop(0, steps)
    def _(s):
        @pl.when(s + AHEAD < steps)
        def _():
            chunk_wait(s, send)
            for to in targets:
                send_copy(s + AHEAD, to).start()

        feet_copy(s).wait()
        chunk_wait(s, recv)
        lanes = pl.ds(pl.multiple_of(s * wide, wide), wide)
        sums[...] += project_step(local, moved[:, :, lanes], feet[s], labels[s], row_ref, col_ref, mix_ref)

    @pl.loop(steps - AHEAD, steps)
    def _(s):
        chunk_wait(s, send)

    frames = groups
    owners = groups * bands
    place = me * bands + pix

    def last_copy(to):
        return pltpu.make_async_remote_copy(
            src_ref=sums.at[pl.ds(pl.multiple_of(to * frames, frames), frames)],
            dst_ref=landed.at[place],
            send_sem=last_send,
            recv_sem=last_recv,
            device_id={"tm": to // bands, "pix": lax.rem(to, bands)},
            device_id_type=mesh_id,
        )

    @pl.loop(0, owners)
    def _(to):
        @pl.when(to != place)
        def _():
            last_copy(to).start()

    landed[place] = sums[pl.ds(pl.multiple_of(place * frames, frames), frames), :]
    taken = landed.at[pl.ds(0, owners - 1)]
    pltpu.make_async_copy(taken, taken, last_recv).wait()
    out_ref[...] = jnp.sum(landed[...], axis=0)
    pltpu.make_async_copy(taken, taken, last_send).wait()


def fused(band, shifts, footprints, ids, groups, bands):
    rows, width = band.shape
    frames = groups
    owners = groups * bands
    steps = width // (GROUP * PATCH)
    foot_cols = footprints.shape[1]
    local = NEURONS // owners
    base = gauss_table(PATCH, pixel_sigma)
    time = gauss_table(frames, frame_sigma)
    full = GROUP * PATCH
    eye = np.eye(GROUP, dtype=np.float32)
    row_table = np.kron(eye, base.astype(np.float32)).astype(ml_dtypes.bfloat16)
    col_table = np.kron(eye, base.astype(np.float32).T).astype(ml_dtypes.bfloat16)
    half = full // frames
    spots = np.eye(half, dtype=np.float32)
    keep = np.einsum("gf,rs->rgfs", np.eye(frames, dtype=np.float32), spots)
    blur = np.einsum("gf,rs->rgfs", time.astype(np.float32), spots)
    mix = np.concatenate([keep.reshape(full, full), -blur.reshape(full, full)], axis=1).astype(ml_dtypes.bfloat16)
    hbm = pl.BlockSpec(memory_space=pltpu.HBM)
    tall = rows + 2 * MAXSHIFT
    bf16, f32, dma = jnp.bfloat16, jnp.float32, pltpu.SemaphoreType.DMA
    count = owners // 2
    return pl.pallas_call(
        lambda *refs: fused_kernel(local, *refs),
        out_shape=jax.ShapeDtypeStruct((frames, local), f32),
        in_specs=[hbm] * 7,
        out_specs=pl.BlockSpec(memory_space=pltpu.VMEM),
        scratch_shapes=[
            pltpu.SMEM(shifts.shape, jnp.int32),
            pltpu.VMEM(ids.shape, jnp.int32),
            pltpu.VMEM((rows, width), bf16),
            pltpu.VMEM((MAXSHIFT, width), bf16),
            pltpu.VMEM((MAXSHIFT, width), bf16),
            pltpu.VMEM((width // TILE + 2, tall, TILE), f32),
            pltpu.VMEM((groups, PATCH, width), bf16),
            pltpu.VMEM((groups, PATCH, width), bf16),
            pltpu.VMEM((steps, GROUP, foot_cols, PATCH * PATCH), bf16),
            pltpu.VMEM(row_table.shape, bf16),
            pltpu.VMEM(col_table.shape, bf16),
            pltpu.VMEM(mix.shape, bf16),
            pltpu.VMEM((steps, 1, GROUP * foot_cols), jnp.int32),
            pltpu.VMEM((owners * frames, local), f32),
            pltpu.VMEM((count * frames, local), f32),
            pltpu.VMEM((count * frames, local), f32),
            pltpu.VMEM((owners, frames, local), f32),
            dma((4,)),
            dma((5,)),
            dma((steps,)),
            dma((2,)),
            dma((2,)),
            dma((steps,)),
            dma((steps,)),
            dma,
            dma,
            dma,
            dma,
            dma,
            pltpu.SemaphoreType.REGULAR,
        ],
        compiler_params=pltpu.CompilerParams(
            vmem_limit_bytes=48 << 20, collective_id=0, has_side_effects=True
        ),
        name="fused",
    )(
        *(
            pltpu.with_memory_space_constraint(operand, pltpu.HBM)
            for operand in (
                shifts,
                band,
                footprints,
                ids,
                jnp.asarray(row_table),
                jnp.asarray(col_table),
                jnp.asarray(mix),
            )
        )
    )


def project_general(moved, footprints, labels, owners):
    frames, side, width = moved.shape
    base = jnp.asarray(gauss_table(side, pixel_sigma))
    time = jnp.asarray(gauss_table(frames, frame_sigma))
    blocks = moved.reshape(frames, side, width // side, side)
    dot = lambda spec, a, b: jnp.einsum(spec, a, b, preferred_element_type=jnp.float32)
    along_rows = dot("ij,fjpc->fipc", base, blocks).astype(jnp.bfloat16)
    along_cols = dot("fipc,dc->fipd", along_rows, base).astype(jnp.bfloat16)
    clean = (blocks.astype(jnp.float32) - dot("gf,fipc->gipc", time, along_cols)).astype(jnp.bfloat16)
    pixels = clean.transpose(2, 0, 1, 3).reshape(width // side, frames, side * side)
    partial = dot("pfx,pkx->fpk", pixels, footprints).reshape(frames, -1)
    wanted = jnp.arange(NEURONS, dtype=jnp.int32)
    onehot = (labels.reshape(-1)[:, None] == wanted[None, :]).astype(jnp.float32)
    sums = jnp.dot(partial, onehot, precision=lax.Precision.HIGHEST, preferred_element_type=jnp.float32)
    return sums.reshape(frames, owners, -1).transpose(1, 0, 2).reshape(owners * frames, -1)


def on_device(movie, shifts, footprints, neuron_ids):
    band = movie[0]
    rows, width = band.shape
    groups = lax.axis_size("tm")
    bands = lax.axis_size("pix")
    owners = groups * bands
    wide = footprints.shape[1] * PATCH
    frames = groups * movie.shape[0]
    fits = (
        frames == groups
        and rows == 4 * TILE
        and rows == groups * PATCH
        and frames * 32 == GROUP * PATCH
        and wide == width
        and bands % 2 == 0
        and NEURONS // owners == LANES
    )
    if fits:
        return fused(band, shifts[0].transpose(0, 2, 1), footprints[0], neuron_ids[0], groups, bands).T
    before, after = halo(band)
    registered = register(band, before, after, shifts)
    slabs = registered.reshape(rows // PATCH, PATCH, width // wide, wide)
    slabs = slabs.transpose(0, 2, 1, 3).reshape(groups, PATCH, wide)
    moved = lax.all_to_all(slabs, "tm", split_axis=0, concat_axis=0, tiled=True)
    sums = project_general(moved, footprints[0], neuron_ids[0], owners)
    sums = lax.all_to_all(
        sums.reshape(owners, frames, -1), ("tm", "pix"), split_axis=0, concat_axis=0, tiled=True
    )
    return jnp.sum(sums, axis=0).T


def solution(mesh):
    in_specs = (
        P("tm", "pix", None),
        P("tm", "pix", None, None),
        P("pix", "tm", None, None),
        P("pix", "tm", None),
    )
    out_specs = P(("tm", "pix"), None)
    return jax.shard_map(
        on_device, mesh=mesh, in_specs=in_specs, out_specs=out_specs, check_vma=False
    )
```

```python
import jax
import jax.numpy as jnp
import ml_dtypes
import numpy as np
from jax import lax
from jax.experimental import pallas as pl
from jax.experimental.pallas import tpu as pltpu
from jax.sharding import PartitionSpec as P

TILE = 128
MAXSHIFT = 16
PATCH = 64
NEURONS = 4096
LANES = 128
GROUP = 4
EARLY = 2
AHEAD = 2
UNIT = 4


pixel_sigma = 3.0
frame_sigma = 4.0


def gauss_table(count, sigma):
    places = np.arange(count).astype(np.float32)
    apart = places[:, None] - places[None, :]
    weights = np.exp(-apart * apart / np.float32(2.0 * sigma * sigma)).astype(np.float32)
    table = weights / np.sum(weights, axis=1, keepdims=True, dtype=np.float32)
    return table.astype(ml_dtypes.bfloat16)


def halo(band):
    count = lax.axis_size("pix")
    up = [(i, i + 1) for i in range(count - 1)]
    down = [(i + 1, i) for i in range(count - 1)]
    before = lax.ppermute(band[-MAXSHIFT:], "pix", up)
    after = lax.ppermute(band[:MAXSHIFT], "pix", down)
    return before, after


def register_kernel(shift_ref, band_ref, before_ref, after_ref, out_ref, padded):
    rows, width = band_ref.shape
    across = width // TILE
    tall = rows + 2 * MAXSHIFT
    for j in (0, across + 1):
        padded[j] = jnp.zeros((tall, TILE), jnp.float32)
    for j in range(across):
        lanes = pl.ds(j * TILE, TILE)
        padded[j + 1, pl.ds(0, MAXSHIFT), :] = before_ref[:, lanes].astype(jnp.float32)
        padded[j + 1, pl.ds(MAXSHIFT, rows), :] = band_ref[:, lanes].astype(jnp.float32)
        padded[j + 1, pl.ds(rows + MAXSHIFT, MAXSHIFT), :] = after_ref[:, lanes].astype(jnp.float32)

    gap = lax.broadcasted_iota(jnp.int32, (2 * TILE, TILE), 0) - lax.broadcasted_iota(
        jnp.int32, (2 * TILE, TILE), 1
    )

    @pl.loop(0, rows // TILE)
    def _(a):
        for b in range(across):
            place = (a * across + b) * 2
            dy = shift_ref[place]
            dx = shift_ref[place + 1]
            left = dx < 0
            start = jnp.where(left, b, b + 1)
            at = pl.ds(a * TILE + MAXSHIFT + dy, TILE)
            window = jnp.concatenate([padded[start, at, :], padded[start + 1, at, :]], axis=1)
            pick = (gap == jnp.where(left, dx + TILE, dx)).astype(jnp.float32).astype(jnp.bfloat16)
            moved = jnp.dot(window.astype(jnp.bfloat16), pick, preferred_element_type=jnp.float32)
            out_ref[pl.ds(pl.multiple_of(a * TILE, TILE), TILE), b * TILE : (b + 1) * TILE] = moved.astype(
                jnp.bfloat16
            )


def register(band, before, after, shifts):
    rows, width = band.shape
    vmem = pl.BlockSpec(memory_space=pltpu.VMEM)
    return pl.pallas_call(
        register_kernel,
        out_shape=jax.ShapeDtypeStruct((rows, width), jnp.bfloat16),
        in_specs=[pl.BlockSpec(memory_space=pltpu.SMEM), vmem, vmem, vmem],
        out_specs=vmem,
        scratch_shapes=[pltpu.VMEM((width // TILE + 2, rows + 2 * MAXSHIFT, TILE), jnp.float32)],
        compiler_params=pltpu.CompilerParams(vmem_limit_bytes=24 << 20),
        name="register",
    )(shifts.reshape(-1), band, before, after)


def project_step(local, x, turned, ids, row_ref, col_ref, mix_ref):
    frames, side, cols = x.shape
    foot_cols = turned.shape[1] // (cols // side)
    half = row_ref.shape[0] // frames
    moved = x.reshape(frames * side, cols)
    chunk = row_ref.shape[0]
    along_rows = jnp.concatenate(
        [
            jnp.dot(row_ref[...], moved[i : i + chunk], preferred_element_type=jnp.float32)
            for i in range(0, frames * side, chunk)
        ],
        axis=0,
    ).astype(jnp.bfloat16)
    along_cols = jnp.dot(along_rows, col_ref[...], preferred_element_type=jnp.float32).astype(jnp.bfloat16)
    patches = cols // side
    low = lax.broadcasted_iota(jnp.int32, (frames, LANES), 1) < side
    pieces = [[] for _ in range(patches)]
    for h in range(side // half):
        stack = [moved[f * side + h * half : f * side + (h + 1) * half] for f in range(frames)]
        stack += [along_cols[f * side + h * half : f * side + (h + 1) * half] for f in range(frames)]
        clean = jnp.dot(mix_ref[...], jnp.concatenate(stack, axis=0), preferred_element_type=jnp.float32)
        for i in range(half // 2):
            for j in range(cols // LANES):
                first = clean[2 * i * frames : (2 * i + 1) * frames, j * LANES : (j + 1) * LANES]
                second = clean[(2 * i + 1) * frames : (2 * i + 2) * frames, j * LANES : (j + 1) * LANES]
                pieces[2 * j].append(jnp.where(low, first, pltpu.roll(second, side, 1)))
                pieces[2 * j + 1].append(jnp.where(low, pltpu.roll(first, side, 1), second))
    pixels = jnp.concatenate([jnp.concatenate(p, axis=1) for p in pieces], axis=0).astype(jnp.bfloat16)
    product = jnp.dot(pixels, turned[...], preferred_element_type=jnp.float32)
    count = product.shape[1]
    owner_patch = lax.broadcasted_iota(jnp.int32, (frames, count), 1) // foot_cols
    partial = jnp.zeros((frames, count), jnp.float32)
    for p in range(patches):
        partial = jnp.where(owner_patch == p, product[p * frames : (p + 1) * frames], partial)
    owner = jnp.broadcast_to(ids // local, (frames, count))
    within = ids % local
    onehot = (
        (lax.broadcasted_iota(jnp.int32, (local, count), 0) == within).astype(jnp.float32).astype(jnp.bfloat16)
    )
    owner_order = range(NEURONS // local)
    total = None
    rest = partial
    for _ in range(3):
        piece = rest.astype(jnp.bfloat16).astype(jnp.float32)
        rest = rest - piece
        spread = jnp.concatenate(
            [jnp.where(owner == o, piece, 0.0) for o in owner_order], axis=0
        ).astype(jnp.bfloat16)
        term = lax.dot_general(spread, onehot, (((1,), (1,)), ((), ())), preferred_element_type=jnp.float32)
        total = term if total is None else total + term
    return total


def fused_kernel(
    local,
    shift_hbm,
    movie_ref,
    foot_ref,
    ids_hbm,
    row_hbm,
    col_hbm,
    mix_hbm,
    out_ref,
    shift_ref,
    ids_ref,
    band,
    before,
    after,
    padded,
    slabs,
    moved,
    feet,
    turned,
    row_ref,
    col_ref,
    mix_ref,
    labels,
    sums,
    other,
    kept,
    landed,
    load,
    table,
    feed,
    halo_send,
    halo_recv,
    send,
    recv,
    here,
    pair_send,
    pair_recv,
    last_send,
    last_recv,
    ready,
):
    groups, side, width = slabs.shape
    steps = feet.shape[0]
    wide = width // steps
    rows = band.shape[0]
    across = width // TILE
    me = lax.axis_index("tm")
    pix = lax.axis_index("pix")
    bands = lax.axis_size("pix")
    half = groups // 2
    upper = me // half
    mesh_id = pl.DeviceIdType.MESH

    per = TILE // side
    last = groups // per - 1
    quarter = me // per
    inside = jnp.logical_and(quarter > 0, quarter < last)

    barrier = pltpu.get_barrier_semaphore()

    def greet(**place):
        pl.semaphore_signal(barrier, inc=1, device_id=place, device_id_type=mesh_id)

    @pl.when(inside)
    def _():
        for e in range(per):
            greet(tm=(last - quarter) * per + e)

    for d in range(1, bands):
        greet(pix=lax.rem(pix + d, bands))
    for t in [*range(per), *range(last * per, groups)]:

        @pl.when(me != t)
        def _():
            greet(tm=t)

    reach = TILE + 2 * MAXSHIFT
    first = jnp.where(upper == 1, TILE - MAXSHIFT, 2 * TILE - MAXSHIFT)
    second = jnp.where(upper == 1, 2 * TILE + MAXSHIFT, TILE - MAXSHIFT)
    ends = TILE - MAXSHIFT
    parts = ((first, reach), (second, TILE), (0, ends), (rows - ends, ends))

    def load_copy(i):
        at = pl.ds(pl.multiple_of(parts[i][0], MAXSHIFT), parts[i][1])
        return pltpu.make_async_copy(movie_ref.at[at], band.at[at], load.at[i])

    table_copies = [
        pltpu.make_async_copy(src, dst, table.at[i])
        for i, (src, dst) in enumerate(
            ((row_hbm, row_ref), (col_hbm, col_ref), (mix_hbm, mix_ref), (ids_hbm, ids_ref))
        )
    ]
    shift_copy = pltpu.make_async_copy(shift_hbm, shift_ref, table.at[4])

    def feet_copy(s):
        return pltpu.make_async_copy(foot_ref.at[pl.ds(s * GROUP, GROUP)], feet.at[s], feed.at[s])

    shift_copy.start()
    for i in range(4):
        load_copy(i).start()
    for copy in table_copies:
        copy.start()

    tall = rows + 2 * MAXSHIFT
    for j in (0, across + 1):
        padded[j] = jnp.zeros((tall, TILE), jnp.float32)

    def widen(i):
        load_copy(i).wait()
        place = pl.multiple_of(parts[i][0], MAXSHIFT)
        for j in range(across):
            lanes = pl.ds(j * TILE, TILE)
            part = band[pl.ds(place, parts[i][1]), lanes]
            padded[j + 1, pl.ds(place + MAXSHIFT, parts[i][1]), :] = part.astype(jnp.float32)

    gap = lax.broadcasted_iota(jnp.int32, (2 * TILE, TILE), 0) - lax.broadcasted_iota(
        jnp.int32, (2 * TILE, TILE), 1
    )

    def register_tiles(a, g):
        for e in range(UNIT):
            b = g * UNIT + e
            dy = shift_ref[a, 0, b]
            dx = shift_ref[a, 1, b]
            left = dx < 0
            start = jnp.where(left, b, b + 1)
            at = pl.ds(a * TILE + MAXSHIFT + dy, TILE)
            window = jnp.concatenate([padded[start, at, :], padded[start + 1, at, :]], axis=1)
            pick = (gap == jnp.where(left, dx + TILE, dx)).astype(jnp.float32).astype(jnp.bfloat16)
            tile = jnp.dot(window.astype(jnp.bfloat16), pick, preferred_element_type=jnp.float32)
            lanes = pl.ds(pl.multiple_of(b * TILE, TILE), TILE)
            slabs[pl.ds(per * a, per), :, lanes] = tile.astype(jnp.bfloat16).reshape(per, side, TILE)

    def tile_row(i):
        up = jnp.where(i == 0, 1, jnp.where(i == 1, 2, jnp.where(i == 2, 0, 3)))
        return jnp.where(upper == 1, up, 3 - up)

    def send_copy(s, to):
        lanes = pl.ds(pl.multiple_of(s * wide, wide), wide)
        return pltpu.make_async_remote_copy(
            src_ref=slabs.at[to, :, lanes],
            dst_ref=moved.at[me, :, lanes],
            send_sem=send.at[s],
            recv_sem=recv.at[s],
            device_id={"tm": to},
            device_id_type=mesh_id,
        )

    def chunk_wait(s, sem):
        lanes = pl.ds(pl.multiple_of(s * wide, wide), wide)
        taken = moved.at[pl.ds(0, groups - 1), :, lanes]
        pltpu.make_async_copy(taken, taken, sem.at[s]).wait()

    def halo_copy(i):
        source = (rows - MAXSHIFT, 0)[i]
        return pltpu.make_async_remote_copy(
            src_ref=movie_ref.at[pl.ds(source, MAXSHIFT)],
            dst_ref=(before, after)[i],
            send_sem=halo_send.at[i],
            recv_sem=halo_recv.at[i],
            device_id={"pix": (pix + 1, pix - 1)[i]},
            device_id_type=mesh_id,
        )

    sends_halo = (pix < bands - 1, pix > 0)
    gets_halo = (pix > 0, pix < bands - 1)

    side_x = lax.rem(me, per)
    mine = (side_x, per - 1 - side_x)
    across_z = {"o": (1 - upper) * last, "i": (1 - upper) + upper * (last // 2)}
    across_z["i"] = 2 - upper
    across_z["o"] = (1 - upper) * last
    inner_z = 1 + upper
    zz = jnp.where(inside, 1, 0)
    across_z["s"] = jnp.where(inside, across_z["i"], across_z["o"])
    across_z["d"] = jnp.where(inside, across_z["o"], across_z["i"])
    other_z = jnp.where(inside, upper * last, inner_z)
    targets = [across_z["o"] * per + mine[1], across_z["i"] * per + mine[1], across_z["o"] * per + mine[0], across_z["i"] * per + mine[0]] + [other_z * per + mine[1], quarter * per + mine[1], other_z * per + mine[0]]

    units = across // UNIT
    nearest = tile_row(0)
    enter = jnp.where(quarter == 0, 2 * units, EARLY * wide // (UNIT * TILE))
    widen(0)
    shift_copy.wait()

    @pl.loop(0, 4 * units)
    def _(u):
        @pl.when(u == enter)
        def _():
            pl.semaphore_wait(barrier, jnp.where(inside, per, groups - 1) + bands - 1)
            for i in range(2):

                @pl.when(sends_halo[i])
                def _():
                    halo_copy(i).start()

            @pl.loop(0, EARLY)
            def _(s):
                for e in range(per):
                    send_copy(s, per * nearest + e).start()

            @pl.when(quarter == last)
            def _():
                for q in range(1, last):
                    to = {"tm": q * per + lax.rem(me, per)}
                    pl.semaphore_signal(ready, inc=1, device_id=to, device_id_type=mesh_id)

        @pl.when(u == 1)
        def _():
            widen(1)

        @pl.when(u == 2 * units)
        def _():
            widen(2)
            widen(3)
            for k in range(2):

                @pl.when(gets_halo[k])
                def _():
                    halo_copy(k).wait_recv()

                @pl.when(jnp.logical_not(gets_halo[k]))
                def _():
                    (before, after)[k][...] = jnp.zeros((MAXSHIFT, width), jnp.bfloat16)

            for j in range(across):
                lanes = pl.ds(j * TILE, TILE)
                padded[j + 1, pl.ds(0, MAXSHIFT), :] = before[:, lanes].astype(jnp.float32)
                padded[j + 1, pl.ds(rows + MAXSHIFT, MAXSHIFT), :] = after[:, lanes].astype(jnp.float32)

        @pl.when(u == 2 * units + 2 * (AHEAD * wide // (UNIT * TILE)))
        def _():
            @pl.when(inside)
            def _():
                pl.semaphore_wait(ready, 1)

            @pl.loop(0, AHEAD)
            def _(s):
                for to in targets:

                    @pl.when(jnp.logical_or(s >= EARLY, to // per != nearest))
                    def _():
                        send_copy(s, to).start()

        v = lax.rem(u, 2 * units)
        register_tiles(tile_row(u // (2 * units) * 2 + lax.rem(v, 2)), v // 2)

    own = pltpu.make_async_copy(slabs.at[me], moved.at[me], here)
    own.start()
    @pl.loop(0, steps)
    def _(s):
        feet_copy(s).start()

    sums[...] = jnp.zeros_like(sums)
    for copy in table_copies:
        copy.wait()
    for s in range(steps):
        labels[s] = jnp.concatenate([ids_ref[p : p + 1, :] for p in range(s * GROUP, (s + 1) * GROUP)], axis=1)
    for i in range(2):

        @pl.when(sends_halo[i])
        def _():
            halo_copy(i).wait_send()

    own.wait()

    @pl.loop(0, steps)
    def _(s):
        @pl.when(s + AHEAD < steps)
        def _():
            chunk_wait(s, send)
            for to in targets:
                send_copy(s + AHEAD, to).start()

        feet_copy(s).wait()
        span = turned.shape[1]
        for c in range(0, turned.shape[0], span):
            turned[c : c + span, :] = feet[s, :, :, c : c + span].reshape(span, span).T

        chunk_wait(s, recv)
        lanes = pl.ds(pl.multiple_of(s * wide, wide), wide)
        sums[...] += project_step(local, moved[:, :, lanes], turned, labels[s], row_ref, col_ref, mix_ref)

    @pl.loop(steps - AHEAD, steps)
    def _(s):
        chunk_wait(s, send)

    frames = groups
    owners = groups * bands
    place = me * bands + pix

    def last_copy(to):
        return pltpu.make_async_remote_copy(
            src_ref=sums.at[pl.ds(pl.multiple_of(to * frames, frames), frames)],
            dst_ref=landed.at[place],
            send_sem=last_send,
            recv_sem=last_recv,
            device_id={"tm": to // bands, "pix": lax.rem(to, bands)},
            device_id_type=mesh_id,
        )

    @pl.loop(0, owners)
    def _(to):
        @pl.when(to != place)
        def _():
            last_copy(to).start()

    landed[place] = sums[pl.ds(pl.multiple_of(place * frames, frames), frames), :]
    taken = landed.at[pl.ds(0, owners - 1)]
    pltpu.make_async_copy(taken, taken, last_recv).wait()
    out_ref[...] = jnp.sum(landed[...], axis=0)
    pltpu.make_async_copy(taken, taken, last_send).wait()


def fused(band, shifts, footprints, ids, groups, bands):
    rows, width = band.shape
    frames = groups
    owners = groups * bands
    steps = width // (GROUP * PATCH)
    foot_cols = footprints.shape[1]
    local = NEURONS // owners
    base = gauss_table(PATCH, pixel_sigma)
    time = gauss_table(frames, frame_sigma)
    full = GROUP * PATCH
    eye = np.eye(GROUP, dtype=np.float32)
    row_table = np.kron(eye, base.astype(np.float32)).astype(ml_dtypes.bfloat16)
    col_table = np.kron(eye, base.astype(np.float32).T).astype(ml_dtypes.bfloat16)
    half = full // frames
    spots = np.eye(half, dtype=np.float32)
    keep = np.einsum("gf,rs->rgfs", np.eye(frames, dtype=np.float32), spots)
    blur = np.einsum("gf,rs->rgfs", time.astype(np.float32), spots)
    mix = np.concatenate([keep.reshape(full, full), -blur.reshape(full, full)], axis=1).astype(ml_dtypes.bfloat16)
    hbm = pl.BlockSpec(memory_space=pltpu.HBM)
    tall = rows + 2 * MAXSHIFT
    bf16, f32, dma = jnp.bfloat16, jnp.float32, pltpu.SemaphoreType.DMA
    count = owners // 2
    return pl.pallas_call(
        lambda *refs: fused_kernel(local, *refs),
        out_shape=jax.ShapeDtypeStruct((frames, local), f32),
        in_specs=[hbm] * 7,
        out_specs=pl.BlockSpec(memory_space=pltpu.VMEM),
        scratch_shapes=[
            pltpu.SMEM(shifts.shape, jnp.int32),
            pltpu.VMEM(ids.shape, jnp.int32),
            pltpu.VMEM((rows, width), bf16),
            pltpu.VMEM((MAXSHIFT, width), bf16),
            pltpu.VMEM((MAXSHIFT, width), bf16),
            pltpu.VMEM((width // TILE + 2, tall, TILE), f32),
            pltpu.VMEM((groups, PATCH, width), bf16),
            pltpu.VMEM((groups, PATCH, width), bf16),
            pltpu.VMEM((steps, GROUP, foot_cols, PATCH * PATCH), bf16),
            pltpu.VMEM((PATCH * PATCH, GROUP * foot_cols), bf16),
            pltpu.VMEM(row_table.shape, bf16),
            pltpu.VMEM(col_table.shape, bf16),
            pltpu.VMEM(mix.shape, bf16),
            pltpu.VMEM((steps, 1, GROUP * foot_cols), jnp.int32),
            pltpu.VMEM((owners * frames, local), f32),
            pltpu.VMEM((count * frames, local), f32),
            pltpu.VMEM((count * frames, local), f32),
            pltpu.VMEM((owners, frames, local), f32),
            dma((4,)),
            dma((5,)),
            dma((steps,)),
            dma((2,)),
            dma((2,)),
            dma((steps,)),
            dma((steps,)),
            dma,
            dma,
            dma,
            dma,
            dma,
            pltpu.SemaphoreType.REGULAR,
        ],
        compiler_params=pltpu.CompilerParams(
            vmem_limit_bytes=48 << 20, collective_id=0, has_side_effects=True
        ),
        name="fused",
    )(
        *(
            pltpu.with_memory_space_constraint(operand, pltpu.HBM)
            for operand in (
                shifts,
                band,
                footprints,
                ids,
                jnp.asarray(row_table),
                jnp.asarray(col_table),
                jnp.asarray(mix),
            )
        )
    )


def project_general(moved, footprints, labels, owners):
    frames, side, width = moved.shape
    base = jnp.asarray(gauss_table(side, pixel_sigma))
    time = jnp.asarray(gauss_table(frames, frame_sigma))
    blocks = moved.reshape(frames, side, width // side, side)
    dot = lambda spec, a, b: jnp.einsum(spec, a, b, preferred_element_type=jnp.float32)
    along_rows = dot("ij,fjpc->fipc", base, blocks).astype(jnp.bfloat16)
    along_cols = dot("fipc,dc->fipd", along_rows, base).astype(jnp.bfloat16)
    clean = (blocks.astype(jnp.float32) - dot("gf,fipc->gipc", time, along_cols)).astype(jnp.bfloat16)
    pixels = clean.transpose(2, 0, 1, 3).reshape(width // side, frames, side * side)
    partial = dot("pfx,pkx->fpk", pixels, footprints).reshape(frames, -1)
    wanted = jnp.arange(NEURONS, dtype=jnp.int32)
    onehot = (labels.reshape(-1)[:, None] == wanted[None, :]).astype(jnp.float32)
    sums = jnp.dot(partial, onehot, precision=lax.Precision.HIGHEST, preferred_element_type=jnp.float32)
    return sums.reshape(frames, owners, -1).transpose(1, 0, 2).reshape(owners * frames, -1)


def on_device(movie, shifts, footprints, neuron_ids):
    band = movie[0]
    rows, width = band.shape
    groups = lax.axis_size("tm")
    bands = lax.axis_size("pix")
    owners = groups * bands
    wide = footprints.shape[1] * PATCH
    frames = groups * movie.shape[0]
    fits = (
        frames == groups
        and rows == 4 * TILE
        and rows == groups * PATCH
        and frames * 32 == GROUP * PATCH
        and wide == width
        and bands % 2 == 0
        and NEURONS // owners == LANES
    )
    if fits:
        return fused(band, shifts[0].transpose(0, 2, 1), footprints[0], neuron_ids[0], groups, bands).T
    before, after = halo(band)
    registered = register(band, before, after, shifts)
    slabs = registered.reshape(rows // PATCH, PATCH, width // wide, wide)
    slabs = slabs.transpose(0, 2, 1, 3).reshape(groups, PATCH, wide)
    moved = lax.all_to_all(slabs, "tm", split_axis=0, concat_axis=0, tiled=True)
    sums = project_general(moved, footprints[0], neuron_ids[0], owners)
    sums = lax.all_to_all(
        sums.reshape(owners, frames, -1), ("tm", "pix"), split_axis=0, concat_axis=0, tiled=True
    )
    return jnp.sum(sums, axis=0).T


def solution(mesh):
    in_specs = (
        P("tm", "pix", None),
        P("tm", "pix", None, None),
        P("pix", "tm", None, None),
        P("pix", "tm", None),
    )
    out_specs = P(("tm", "pix"), None)
    return jax.shard_map(
        on_device, mesh=mesh, in_specs=in_specs, out_specs=out_specs, check_vma=False
    )
```

```python
import jax
import jax.numpy as jnp
import ml_dtypes
import numpy as np
from jax import lax
from jax.experimental import pallas as pl
from jax.experimental.pallas import tpu as pltpu
from jax.sharding import PartitionSpec as P

TILE = 128
MAXSHIFT = 16
PATCH = 64
NEURONS = 4096
LANES = 128
GROUP = 4
EARLY = 2
AHEAD = 2
UNIT = 4


pixel_sigma = 3.0
frame_sigma = 4.0


def gauss_table(count, sigma):
    places = np.arange(count).astype(np.float32)
    apart = places[:, None] - places[None, :]
    weights = np.exp(-apart * apart / np.float32(2.0 * sigma * sigma)).astype(np.float32)
    table = weights / np.sum(weights, axis=1, keepdims=True, dtype=np.float32)
    return table.astype(ml_dtypes.bfloat16)


def halo(band):
    count = lax.axis_size("pix")
    up = [(i, i + 1) for i in range(count - 1)]
    down = [(i + 1, i) for i in range(count - 1)]
    before = lax.ppermute(band[-MAXSHIFT:], "pix", up)
    after = lax.ppermute(band[:MAXSHIFT], "pix", down)
    return before, after


def register_kernel(shift_ref, band_ref, before_ref, after_ref, out_ref, padded):
    rows, width = band_ref.shape
    across = width // TILE
    tall = rows + 2 * MAXSHIFT
    for j in (0, across + 1):
        padded[j] = jnp.zeros((tall, TILE), jnp.float32)
    for j in range(across):
        lanes = pl.ds(j * TILE, TILE)
        padded[j + 1, pl.ds(0, MAXSHIFT), :] = before_ref[:, lanes].astype(jnp.float32)
        padded[j + 1, pl.ds(MAXSHIFT, rows), :] = band_ref[:, lanes].astype(jnp.float32)
        padded[j + 1, pl.ds(rows + MAXSHIFT, MAXSHIFT), :] = after_ref[:, lanes].astype(jnp.float32)

    gap = lax.broadcasted_iota(jnp.int32, (2 * TILE, TILE), 0) - lax.broadcasted_iota(
        jnp.int32, (2 * TILE, TILE), 1
    )

    @pl.loop(0, rows // TILE)
    def _(a):
        for b in range(across):
            place = (a * across + b) * 2
            dy = shift_ref[place]
            dx = shift_ref[place + 1]
            left = dx < 0
            start = jnp.where(left, b, b + 1)
            at = pl.ds(a * TILE + MAXSHIFT + dy, TILE)
            window = jnp.concatenate([padded[start, at, :], padded[start + 1, at, :]], axis=1)
            pick = (gap == jnp.where(left, dx + TILE, dx)).astype(jnp.float32).astype(jnp.bfloat16)
            moved = jnp.dot(window.astype(jnp.bfloat16), pick, preferred_element_type=jnp.float32)
            out_ref[pl.ds(pl.multiple_of(a * TILE, TILE), TILE), b * TILE : (b + 1) * TILE] = moved.astype(
                jnp.bfloat16
            )


def register(band, before, after, shifts):
    rows, width = band.shape
    vmem = pl.BlockSpec(memory_space=pltpu.VMEM)
    return pl.pallas_call(
        register_kernel,
        out_shape=jax.ShapeDtypeStruct((rows, width), jnp.bfloat16),
        in_specs=[pl.BlockSpec(memory_space=pltpu.SMEM), vmem, vmem, vmem],
        out_specs=vmem,
        scratch_shapes=[pltpu.VMEM((width // TILE + 2, rows + 2 * MAXSHIFT, TILE), jnp.float32)],
        compiler_params=pltpu.CompilerParams(vmem_limit_bytes=24 << 20),
        name="register",
    )(shifts.reshape(-1), band, before, after)


def project_step(local, x, turned, ids, onehot, row_ref, col_ref, mix_ref):
    frames, side, cols = x.shape
    foot_cols = turned.shape[1] // (cols // side)
    half = row_ref.shape[0] // frames
    moved = x.reshape(frames * side, cols)
    chunk = row_ref.shape[0]
    along_rows = jnp.concatenate(
        [
            jnp.dot(row_ref[...], moved[i : i + chunk], preferred_element_type=jnp.float32)
            for i in range(0, frames * side, chunk)
        ],
        axis=0,
    ).astype(jnp.bfloat16)
    along_cols = jnp.dot(along_rows, col_ref[...], preferred_element_type=jnp.float32).astype(jnp.bfloat16)
    patches = cols // side
    low = lax.broadcasted_iota(jnp.int32, (frames, LANES), 1) < side
    pieces = [[] for _ in range(patches)]
    for h in range(side // half):
        stack = [moved[f * side + h * half : f * side + (h + 1) * half] for f in range(frames)]
        stack += [along_cols[f * side + h * half : f * side + (h + 1) * half] for f in range(frames)]
        clean = jnp.dot(mix_ref[...], jnp.concatenate(stack, axis=0), preferred_element_type=jnp.float32)
        for i in range(half // 2):
            for j in range(cols // LANES):
                first = clean[2 * i * frames : (2 * i + 1) * frames, j * LANES : (j + 1) * LANES]
                second = clean[(2 * i + 1) * frames : (2 * i + 2) * frames, j * LANES : (j + 1) * LANES]
                pieces[2 * j].append(jnp.where(low, first, pltpu.roll(second, side, 1)))
                pieces[2 * j + 1].append(jnp.where(low, pltpu.roll(first, side, 1), second))
    pixels = jnp.concatenate([jnp.concatenate(p, axis=1) for p in pieces], axis=0).astype(jnp.bfloat16)
    product = jnp.dot(pixels, turned[...], preferred_element_type=jnp.float32)
    count = product.shape[1]
    owner_patch = lax.broadcasted_iota(jnp.int32, (frames, count), 1) // foot_cols
    partial = jnp.zeros((frames, count), jnp.float32)
    for p in range(patches):
        partial = jnp.where(owner_patch == p, product[p * frames : (p + 1) * frames], partial)
    owner = jnp.broadcast_to(ids // local, (frames, count))
    owner_order = range(NEURONS // local)
    total = None
    rest = partial
    for _ in range(3):
        piece = rest.astype(jnp.bfloat16).astype(jnp.float32)
        rest = rest - piece
        spread = jnp.concatenate(
            [jnp.where(owner == o, piece, 0.0) for o in owner_order], axis=0
        ).astype(jnp.bfloat16)
        term = jnp.dot(spread, onehot[...], preferred_element_type=jnp.float32)
        total = term if total is None else total + term
    return total


def fused_kernel(
    local,
    shift_hbm,
    movie_ref,
    foot_ref,
    ids_hbm,
    row_hbm,
    col_hbm,
    mix_hbm,
    out_ref,
    shift_ref,
    ids_ref,
    band,
    before,
    after,
    padded,
    slabs,
    moved,
    feet,
    turned,
    onehot,
    row_ref,
    col_ref,
    mix_ref,
    labels,
    sums,
    landed,
    load,
    table,
    feed,
    halo_send,
    halo_recv,
    send,
    recv,
    here,
    last_send,
    last_recv,
    ready,
):
    groups, side, width = slabs.shape
    steps = feet.shape[0]
    wide = width // steps
    rows = band.shape[0]
    across = width // TILE
    me = lax.axis_index("tm")
    pix = lax.axis_index("pix")
    bands = lax.axis_size("pix")
    upper = me // (groups // 2)
    mesh_id = pl.DeviceIdType.MESH

    per = TILE // side
    last = groups // per - 1
    quarter = me // per
    inside = jnp.logical_and(quarter > 0, quarter < last)

    barrier = pltpu.get_barrier_semaphore()

    def greet(**place):
        pl.semaphore_signal(barrier, inc=1, device_id=place, device_id_type=mesh_id)

    @pl.when(inside)
    def _():
        for e in range(per):
            greet(tm=(last - quarter) * per + e)

    for d in range(1, bands):
        greet(pix=lax.rem(pix + d, bands))
    for t in [*range(per), *range(last * per, groups)]:

        @pl.when(me != t)
        def _():
            greet(tm=t)

    reach = TILE + 2 * MAXSHIFT
    first = jnp.where(upper == 1, TILE - MAXSHIFT, 2 * TILE - MAXSHIFT)
    second = jnp.where(upper == 1, 2 * TILE + MAXSHIFT, TILE - MAXSHIFT)
    ends = TILE - MAXSHIFT
    parts = ((first, reach), (second, TILE), (0, ends), (rows - ends, ends))

    def load_copy(i):
        at = pl.ds(pl.multiple_of(parts[i][0], MAXSHIFT), parts[i][1])
        return pltpu.make_async_copy(movie_ref.at[at], band.at[at], load.at[i])

    table_copies = [
        pltpu.make_async_copy(src, dst, table.at[i])
        for i, (src, dst) in enumerate(
            ((row_hbm, row_ref), (col_hbm, col_ref), (mix_hbm, mix_ref), (ids_hbm, ids_ref))
        )
    ]
    shift_copy = pltpu.make_async_copy(shift_hbm, shift_ref, table.at[4])

    def feet_copy(s):
        return pltpu.make_async_copy(foot_ref.at[pl.ds(s * GROUP, GROUP)], feet.at[s], feed.at[s])

    shift_copy.start()
    for i in range(4):
        load_copy(i).start()
    for copy in table_copies:
        copy.start()

    tall = rows + 2 * MAXSHIFT
    for j in (0, across + 1):
        padded[j] = jnp.zeros((tall, TILE), jnp.float32)

    def widen(i):
        load_copy(i).wait()
        place = pl.multiple_of(parts[i][0], MAXSHIFT)
        for j in range(across):
            lanes = pl.ds(j * TILE, TILE)
            part = band[pl.ds(place, parts[i][1]), lanes]
            padded[j + 1, pl.ds(place + MAXSHIFT, parts[i][1]), :] = part.astype(jnp.float32)

    gap = lax.broadcasted_iota(jnp.int32, (2 * TILE, TILE), 0) - lax.broadcasted_iota(
        jnp.int32, (2 * TILE, TILE), 1
    )

    def register_tiles(a, g):
        for e in range(UNIT):
            b = g * UNIT + e
            dy = shift_ref[a, 0, b]
            dx = shift_ref[a, 1, b]
            left = dx < 0
            start = jnp.where(left, b, b + 1)
            at = pl.ds(a * TILE + MAXSHIFT + dy, TILE)
            window = jnp.concatenate([padded[start, at, :], padded[start + 1, at, :]], axis=1)
            pick = (gap == jnp.where(left, dx + TILE, dx)).astype(jnp.float32).astype(jnp.bfloat16)
            tile = jnp.dot(window.astype(jnp.bfloat16), pick, preferred_element_type=jnp.float32)
            lanes = pl.ds(pl.multiple_of(b * TILE, TILE), TILE)
            slabs[pl.ds(per * a, per), :, lanes] = tile.astype(jnp.bfloat16).reshape(per, side, TILE)

    def tile_row(i):
        up = jnp.where(i == 0, 1, jnp.where(i == 1, 2, jnp.where(i == 2, 0, 3)))
        return jnp.where(upper == 1, up, 3 - up)

    def send_copy(s, to):
        lanes = pl.ds(pl.multiple_of(s * wide, wide), wide)
        return pltpu.make_async_remote_copy(
            src_ref=slabs.at[to, :, lanes],
            dst_ref=moved.at[me, :, lanes],
            send_sem=send.at[s],
            recv_sem=recv.at[s],
            device_id={"tm": to},
            device_id_type=mesh_id,
        )

    def chunk_wait(s, sem):
        lanes = pl.ds(pl.multiple_of(s * wide, wide), wide)
        taken = moved.at[pl.ds(0, groups - 1), :, lanes]
        pltpu.make_async_copy(taken, taken, sem.at[s]).wait()

    def halo_copy(i):
        source = (rows - MAXSHIFT, 0)[i]
        return pltpu.make_async_remote_copy(
            src_ref=movie_ref.at[pl.ds(source, MAXSHIFT)],
            dst_ref=(before, after)[i],
            send_sem=halo_send.at[i],
            recv_sem=halo_recv.at[i],
            device_id={"pix": (pix + 1, pix - 1)[i]},
            device_id_type=mesh_id,
        )

    sends_halo = (pix < bands - 1, pix > 0)
    gets_halo = (pix > 0, pix < bands - 1)

    side_x = lax.rem(me, per)
    mine = (side_x, per - 1 - side_x)
    outer_z = (1 - upper) * last
    inner_z = 2 - upper
    other_z = jnp.where(inside, upper * last, 1 + upper)
    targets = [z * per + x for x in (mine[1], mine[0]) for z in (outer_z, inner_z)]
    targets += [other_z * per + mine[1], quarter * per + mine[1], other_z * per + mine[0]]

    units = across // UNIT
    nearest = tile_row(0)
    enter = jnp.where(quarter == 0, 2 * units, EARLY * wide // (UNIT * TILE))
    widen(0)
    shift_copy.wait()

    @pl.loop(0, 4 * units)
    def _(u):
        @pl.when(u == enter)
        def _():
            pl.semaphore_wait(barrier, jnp.where(inside, per, groups - 1) + bands - 1)
            for i in range(2):

                @pl.when(sends_halo[i])
                def _():
                    halo_copy(i).start()

            @pl.loop(0, EARLY)
            def _(s):
                for e in range(per):
                    send_copy(s, per * nearest + e).start()

            @pl.when(quarter == last)
            def _():
                for q in range(1, last):
                    to = {"tm": q * per + lax.rem(me, per)}
                    pl.semaphore_signal(ready, inc=1, device_id=to, device_id_type=mesh_id)

        @pl.when(u == 1)
        def _():
            widen(1)

        @pl.when(u == 2 * units)
        def _():
            widen(2)
            widen(3)
            for k in range(2):

                @pl.when(gets_halo[k])
                def _():
                    halo_copy(k).wait_recv()

                @pl.when(jnp.logical_not(gets_halo[k]))
                def _():
                    (before, after)[k][...] = jnp.zeros((MAXSHIFT, width), jnp.bfloat16)

            for j in range(across):
                lanes = pl.ds(j * TILE, TILE)
                padded[j + 1, pl.ds(0, MAXSHIFT), :] = before[:, lanes].astype(jnp.float32)
                padded[j + 1, pl.ds(rows + MAXSHIFT, MAXSHIFT), :] = after[:, lanes].astype(jnp.float32)

        @pl.when(u == 2 * units + 2 * (AHEAD * wide // (UNIT * TILE)))
        def _():
            @pl.when(inside)
            def _():
                pl.semaphore_wait(ready, 1)

            @pl.loop(0, AHEAD)
            def _(s):
                for to in targets:

                    @pl.when(jnp.logical_or(s >= EARLY, to // per != nearest))
                    def _():
                        send_copy(s, to).start()

        v = lax.rem(u, 2 * units)
        register_tiles(tile_row(u // (2 * units) * 2 + lax.rem(v, 2)), v // 2)

    own = pltpu.make_async_copy(slabs.at[me], moved.at[me], here)
    own.start()

    @pl.loop(0, steps)
    def _(s):
        feet_copy(s).start()

    sums[...] = jnp.zeros_like(sums)
    for copy in table_copies:
        copy.wait()
    for s in range(steps):
        labels[s] = jnp.concatenate([ids_ref[p : p + 1, :] for p in range(s * GROUP, (s + 1) * GROUP)], axis=1)
    for i in range(2):

        @pl.when(sends_halo[i])
        def _():
            halo_copy(i).wait_send()

    own.wait()

    @pl.loop(0, steps)
    def _(s):
        @pl.when(s + AHEAD < steps)
        def _():
            chunk_wait(s, send)
            for to in targets:
                send_copy(s + AHEAD, to).start()

        feet_copy(s).wait()
        span = turned.shape[1]
        within = labels[s] % local
        places = lax.broadcasted_iota(jnp.int32, (local, span), 0)
        onehot[...] = (places == within).astype(jnp.float32).astype(jnp.bfloat16).T
        for c in range(0, turned.shape[0], span):
            turned[c : c + span, :] = feet[s, :, :, c : c + span].reshape(span, span).T

        chunk_wait(s, recv)
        lanes = pl.ds(pl.multiple_of(s * wide, wide), wide)
        sums[...] += project_step(local, moved[:, :, lanes], turned, labels[s], onehot, row_ref, col_ref, mix_ref)

    frames = groups
    owners = groups * bands
    place = me * bands + pix

    def last_copy(to):
        return pltpu.make_async_remote_copy(
            src_ref=sums.at[pl.ds(pl.multiple_of(to * frames, frames), frames)],
            dst_ref=landed.at[place],
            send_sem=last_send,
            recv_sem=last_recv,
            device_id={"tm": to // bands, "pix": lax.rem(to, bands)},
            device_id_type=mesh_id,
        )

    @pl.loop(0, owners)
    def _(to):
        @pl.when(to != place)
        def _():
            last_copy(to).start()

    landed[place] = sums[pl.ds(pl.multiple_of(place * frames, frames), frames), :]

    @pl.loop(steps - AHEAD, steps)
    def _(s):
        chunk_wait(s, send)

    taken = landed.at[pl.ds(0, owners - 1)]
    pltpu.make_async_copy(taken, taken, last_recv).wait()
    out_ref[...] = jnp.sum(landed[...], axis=0)
    pltpu.make_async_copy(taken, taken, last_send).wait()


def fused(band, shifts, footprints, ids, groups, bands):
    rows, width = band.shape
    frames = groups
    owners = groups * bands
    steps = width // (GROUP * PATCH)
    foot_cols = footprints.shape[1]
    local = NEURONS // owners
    base = gauss_table(PATCH, pixel_sigma)
    time = gauss_table(frames, frame_sigma)
    full = GROUP * PATCH
    eye = np.eye(GROUP, dtype=np.float32)
    row_table = np.kron(eye, base.astype(np.float32)).astype(ml_dtypes.bfloat16)
    col_table = np.kron(eye, base.astype(np.float32).T).astype(ml_dtypes.bfloat16)
    half = full // frames
    spots = np.eye(half, dtype=np.float32)
    keep = np.einsum("gf,rs->rgfs", np.eye(frames, dtype=np.float32), spots)
    blur = np.einsum("gf,rs->rgfs", time.astype(np.float32), spots)
    mix = np.concatenate([keep.reshape(full, full), -blur.reshape(full, full)], axis=1).astype(ml_dtypes.bfloat16)
    hbm = pl.BlockSpec(memory_space=pltpu.HBM)
    tall = rows + 2 * MAXSHIFT
    bf16, f32, dma = jnp.bfloat16, jnp.float32, pltpu.SemaphoreType.DMA
    return pl.pallas_call(
        lambda *refs: fused_kernel(local, *refs),
        out_shape=jax.ShapeDtypeStruct((frames, local), f32),
        in_specs=[hbm] * 7,
        out_specs=pl.BlockSpec(memory_space=pltpu.VMEM),
        scratch_shapes=[
            pltpu.SMEM(shifts.shape, jnp.int32),
            pltpu.VMEM(ids.shape, jnp.int32),
            pltpu.VMEM((rows, width), bf16),
            pltpu.VMEM((MAXSHIFT, width), bf16),
            pltpu.VMEM((MAXSHIFT, width), bf16),
            pltpu.VMEM((width // TILE + 2, tall, TILE), f32),
            pltpu.VMEM((groups, PATCH, width), bf16),
            pltpu.VMEM((groups, PATCH, width), bf16),
            pltpu.VMEM((steps, GROUP, foot_cols, PATCH * PATCH), bf16),
            pltpu.VMEM((PATCH * PATCH, GROUP * foot_cols), bf16),
            pltpu.VMEM((GROUP * foot_cols, local), bf16),
            pltpu.VMEM(row_table.shape, bf16),
            pltpu.VMEM(col_table.shape, bf16),
            pltpu.VMEM(mix.shape, bf16),
            pltpu.VMEM((steps, 1, GROUP * foot_cols), jnp.int32),
            pltpu.VMEM((owners * frames, local), f32),
            pltpu.VMEM((owners, frames, local), f32),
            dma((4,)),
            dma((5,)),
            dma((steps,)),
            dma((2,)),
            dma((2,)),
            dma((steps,)),
            dma((steps,)),
            dma,
            dma,
            dma,
            pltpu.SemaphoreType.REGULAR,
        ],
        compiler_params=pltpu.CompilerParams(
            vmem_limit_bytes=48 << 20, collective_id=0, has_side_effects=True
        ),
        name="fused",
    )(
        *(
            pltpu.with_memory_space_constraint(operand, pltpu.HBM)
            for operand in (
                shifts,
                band,
                footprints,
                ids,
                jnp.asarray(row_table),
                jnp.asarray(col_table),
                jnp.asarray(mix),
            )
        )
    )


def project_general(moved, footprints, labels, owners):
    frames, side, width = moved.shape
    base = jnp.asarray(gauss_table(side, pixel_sigma))
    time = jnp.asarray(gauss_table(frames, frame_sigma))
    blocks = moved.reshape(frames, side, width // side, side)
    dot = lambda spec, a, b: jnp.einsum(spec, a, b, preferred_element_type=jnp.float32)
    along_rows = dot("ij,fjpc->fipc", base, blocks).astype(jnp.bfloat16)
    along_cols = dot("fipc,dc->fipd", along_rows, base).astype(jnp.bfloat16)
    clean = (blocks.astype(jnp.float32) - dot("gf,fipc->gipc", time, along_cols)).astype(jnp.bfloat16)
    pixels = clean.transpose(2, 0, 1, 3).reshape(width // side, frames, side * side)
    partial = dot("pfx,pkx->fpk", pixels, footprints).reshape(frames, -1)
    wanted = jnp.arange(NEURONS, dtype=jnp.int32)
    onehot = (labels.reshape(-1)[:, None] == wanted[None, :]).astype(jnp.float32)
    sums = jnp.dot(partial, onehot, precision=lax.Precision.HIGHEST, preferred_element_type=jnp.float32)
    return sums.reshape(frames, owners, -1).transpose(1, 0, 2).reshape(owners * frames, -1)


def on_device(movie, shifts, footprints, neuron_ids):
    band = movie[0]
    rows, width = band.shape
    groups = lax.axis_size("tm")
    bands = lax.axis_size("pix")
    owners = groups * bands
    wide = footprints.shape[1] * PATCH
    frames = groups * movie.shape[0]
    fits = (
        frames == groups
        and rows == 4 * TILE
        and rows == groups * PATCH
        and frames * 32 == GROUP * PATCH
        and wide == width
        and NEURONS // owners == LANES
    )
    if fits:
        return fused(band, shifts[0].transpose(0, 2, 1), footprints[0], neuron_ids[0], groups, bands).T
    before, after = halo(band)
    registered = register(band, before, after, shifts)
    slabs = registered.reshape(rows // PATCH, PATCH, width // wide, wide)
    slabs = slabs.transpose(0, 2, 1, 3).reshape(groups, PATCH, wide)
    moved = lax.all_to_all(slabs, "tm", split_axis=0, concat_axis=0, tiled=True)
    sums = project_general(moved, footprints[0], neuron_ids[0], owners)
    sums = lax.all_to_all(
        sums.reshape(owners, frames, -1), ("tm", "pix"), split_axis=0, concat_axis=0, tiled=True
    )
    return jnp.sum(sums, axis=0).T


def solution(mesh):
    in_specs = (
        P("tm", "pix", None),
        P("tm", "pix", None, None),
        P("pix", "tm", None, None),
        P("pix", "tm", None),
    )
    out_specs = P(("tm", "pix"), None)
    return jax.shard_map(
        on_device, mesh=mesh, in_specs=in_specs, out_specs=out_specs, check_vma=False
    )
```

```python
import jax
import jax.numpy as jnp
import ml_dtypes
import numpy as np
from jax import lax
from jax.experimental import pallas as pl
from jax.experimental.pallas import tpu as pltpu
from jax.sharding import PartitionSpec as P

TILE = 128
MAXSHIFT = 16
PATCH = 64
NEURONS = 4096
LANES = 128
GROUP = 4
EARLY = 2
AHEAD = 2
UNIT = 4


pixel_sigma = 3.0
frame_sigma = 4.0


def gauss_table(count, sigma):
    places = np.arange(count).astype(np.float32)
    apart = places[:, None] - places[None, :]
    weights = np.exp(-apart * apart / np.float32(2.0 * sigma * sigma)).astype(np.float32)
    table = weights / np.sum(weights, axis=1, keepdims=True, dtype=np.float32)
    return table.astype(ml_dtypes.bfloat16)


def halo(band):
    count = lax.axis_size("pix")
    up = [(i, i + 1) for i in range(count - 1)]
    down = [(i + 1, i) for i in range(count - 1)]
    before = lax.ppermute(band[-MAXSHIFT:], "pix", up)
    after = lax.ppermute(band[:MAXSHIFT], "pix", down)
    return before, after


def register_kernel(shift_ref, band_ref, before_ref, after_ref, out_ref, padded):
    rows, width = band_ref.shape
    across = width // TILE
    tall = rows + 2 * MAXSHIFT
    for j in (0, across + 1):
        padded[j] = jnp.zeros((tall, TILE), jnp.float32)
    for j in range(across):
        lanes = pl.ds(j * TILE, TILE)
        padded[j + 1, pl.ds(0, MAXSHIFT), :] = before_ref[:, lanes].astype(jnp.float32)
        padded[j + 1, pl.ds(MAXSHIFT, rows), :] = band_ref[:, lanes].astype(jnp.float32)
        padded[j + 1, pl.ds(rows + MAXSHIFT, MAXSHIFT), :] = after_ref[:, lanes].astype(jnp.float32)

    gap = lax.broadcasted_iota(jnp.int32, (2 * TILE, TILE), 0) - lax.broadcasted_iota(
        jnp.int32, (2 * TILE, TILE), 1
    )

    @pl.loop(0, rows // TILE)
    def _(a):
        for b in range(across):
            place = (a * across + b) * 2
            dy = shift_ref[place]
            dx = shift_ref[place + 1]
            left = dx < 0
            start = jnp.where(left, b, b + 1)
            at = pl.ds(a * TILE + MAXSHIFT + dy, TILE)
            window = jnp.concatenate([padded[start, at, :], padded[start + 1, at, :]], axis=1)
            pick = (gap == jnp.where(left, dx + TILE, dx)).astype(jnp.float32).astype(jnp.bfloat16)
            moved = jnp.dot(window.astype(jnp.bfloat16), pick, preferred_element_type=jnp.float32)
            out_ref[pl.ds(pl.multiple_of(a * TILE, TILE), TILE), b * TILE : (b + 1) * TILE] = moved.astype(
                jnp.bfloat16
            )


def register(band, before, after, shifts):
    rows, width = band.shape
    vmem = pl.BlockSpec(memory_space=pltpu.VMEM)
    return pl.pallas_call(
        register_kernel,
        out_shape=jax.ShapeDtypeStruct((rows, width), jnp.bfloat16),
        in_specs=[pl.BlockSpec(memory_space=pltpu.SMEM), vmem, vmem, vmem],
        out_specs=vmem,
        scratch_shapes=[pltpu.VMEM((width // TILE + 2, rows + 2 * MAXSHIFT, TILE), jnp.float32)],
        compiler_params=pltpu.CompilerParams(vmem_limit_bytes=24 << 20),
        name="register",
    )(shifts.reshape(-1), band, before, after)


def project_step(local, x, turned, ids, onehot, row_ref, col_ref, mix_ref):
    frames, side, cols = x.shape
    foot_cols = turned.shape[1] // (cols // side)
    half = row_ref.shape[0] // frames
    moved = x.reshape(frames * side, cols)
    chunk = row_ref.shape[0]
    along_rows = jnp.concatenate(
        [
            jnp.dot(row_ref[...], moved[i : i + chunk], preferred_element_type=jnp.float32)
            for i in range(0, frames * side, chunk)
        ],
        axis=0,
    ).astype(jnp.bfloat16)
    along_cols = jnp.dot(along_rows, col_ref[...], preferred_element_type=jnp.float32).astype(jnp.bfloat16)
    patches = cols // side
    low = lax.broadcasted_iota(jnp.int32, (frames, LANES), 1) < side
    pieces = [[] for _ in range(patches)]
    for h in range(side // half):
        stack = [moved[f * side + h * half : f * side + (h + 1) * half] for f in range(frames)]
        stack += [along_cols[f * side + h * half : f * side + (h + 1) * half] for f in range(frames)]
        clean = jnp.dot(mix_ref[...], jnp.concatenate(stack, axis=0), preferred_element_type=jnp.float32)
        for i in range(half // 2):
            for j in range(cols // LANES):
                first = clean[2 * i * frames : (2 * i + 1) * frames, j * LANES : (j + 1) * LANES]
                second = clean[(2 * i + 1) * frames : (2 * i + 2) * frames, j * LANES : (j + 1) * LANES]
                pieces[2 * j].append(jnp.where(low, first, pltpu.roll(second, side, 1)))
                pieces[2 * j + 1].append(jnp.where(low, pltpu.roll(first, side, 1), second))
    pixels = jnp.concatenate([jnp.concatenate(p, axis=1) for p in pieces], axis=0).astype(jnp.bfloat16)
    product = jnp.dot(pixels, turned[...], preferred_element_type=jnp.float32)
    count = product.shape[1]
    owner_patch = lax.broadcasted_iota(jnp.int32, (frames, count), 1) // foot_cols
    partial = jnp.zeros((frames, count), jnp.float32)
    for p in range(patches):
        partial = jnp.where(owner_patch == p, product[p * frames : (p + 1) * frames], partial)
    owner = jnp.broadcast_to(ids // local, (frames, count))
    owner_order = range(NEURONS // local)
    total = None
    rest = partial
    for _ in range(3):
        piece = rest.astype(jnp.bfloat16).astype(jnp.float32)
        rest = rest - piece
        spread = jnp.concatenate(
            [jnp.where(owner == o, piece, 0.0) for o in owner_order], axis=0
        ).astype(jnp.bfloat16)
        term = jnp.dot(spread, onehot[...], preferred_element_type=jnp.float32)
        total = term if total is None else total + term
    return total


def fused_kernel(
    local,
    shift_hbm,
    movie_ref,
    foot_ref,
    ids_hbm,
    row_hbm,
    col_hbm,
    mix_hbm,
    out_ref,
    shift_ref,
    ids_ref,
    band,
    before,
    after,
    padded,
    slabs,
    moved,
    feet,
    turned,
    onehot,
    row_ref,
    col_ref,
    mix_ref,
    labels,
    sums,
    landed,
    load,
    table,
    feed,
    halo_send,
    halo_recv,
    send,
    recv,
    here,
    last_send,
    last_recv,
    ready,
):
    groups, side, width = slabs.shape
    steps = feet.shape[0]
    wide = width // steps
    rows = band.shape[0]
    across = width // TILE
    me = lax.axis_index("tm")
    pix = lax.axis_index("pix")
    bands = lax.axis_size("pix")
    upper = me // (groups // 2)
    mesh_id = pl.DeviceIdType.MESH

    per = TILE // side
    last = groups // per - 1
    quarter = me // per
    inside = jnp.logical_and(quarter > 0, quarter < last)

    barrier = pltpu.get_barrier_semaphore()

    def greet(**place):
        pl.semaphore_signal(barrier, inc=1, device_id=place, device_id_type=mesh_id)

    @pl.when(inside)
    def _():
        for e in range(per):
            greet(tm=(last - quarter) * per + e)

    for d in range(1, bands):
        greet(pix=lax.rem(pix + d, bands))
    for t in [*range(per), *range(last * per, groups)]:

        @pl.when(me != t)
        def _():
            greet(tm=t)

    reach = TILE + 2 * MAXSHIFT
    first = jnp.where(upper == 1, TILE - MAXSHIFT, 2 * TILE - MAXSHIFT)
    second = jnp.where(upper == 1, 2 * TILE + MAXSHIFT, TILE - MAXSHIFT)
    ends = TILE - MAXSHIFT
    parts = ((first, reach), (second, TILE), (0, ends), (rows - ends, ends))

    def load_copy(i):
        at = pl.ds(pl.multiple_of(parts[i][0], MAXSHIFT), parts[i][1])
        return pltpu.make_async_copy(movie_ref.at[at], band.at[at], load.at[i])

    table_copies = [
        pltpu.make_async_copy(src, dst, table.at[i])
        for i, (src, dst) in enumerate(
            ((row_hbm, row_ref), (col_hbm, col_ref), (mix_hbm, mix_ref), (ids_hbm, ids_ref))
        )
    ]
    shift_copy = pltpu.make_async_copy(shift_hbm, shift_ref, table.at[4])

    def feet_copy(s):
        return pltpu.make_async_copy(foot_ref.at[pl.ds(s * GROUP, GROUP)], feet.at[s], feed.at[s])

    shift_copy.start()
    for i in range(4):
        load_copy(i).start()
    for copy in table_copies:
        copy.start()

    tall = rows + 2 * MAXSHIFT
    for j in (0, across + 1):
        padded[j] = jnp.zeros((tall, TILE), jnp.float32)

    def widen(i):
        load_copy(i).wait()
        place = pl.multiple_of(parts[i][0], MAXSHIFT)
        for j in range(across):
            lanes = pl.ds(j * TILE, TILE)
            part = band[pl.ds(place, parts[i][1]), lanes]
            padded[j + 1, pl.ds(place + MAXSHIFT, parts[i][1]), :] = part.astype(jnp.float32)

    gap = lax.broadcasted_iota(jnp.int32, (2 * TILE, TILE), 0) - lax.broadcasted_iota(
        jnp.int32, (2 * TILE, TILE), 1
    )

    def register_tiles(a, g):
        for e in range(UNIT):
            b = g * UNIT + e
            dy = shift_ref[a, 0, b]
            dx = shift_ref[a, 1, b]
            left = dx < 0
            start = jnp.where(left, b, b + 1)
            at = pl.ds(a * TILE + MAXSHIFT + dy, TILE)
            window = jnp.concatenate([padded[start, at, :], padded[start + 1, at, :]], axis=1)
            pick = (gap == jnp.where(left, dx + TILE, dx)).astype(jnp.float32).astype(jnp.bfloat16)
            tile = jnp.dot(window.astype(jnp.bfloat16), pick, preferred_element_type=jnp.float32)
            lanes = pl.ds(pl.multiple_of(b * TILE, TILE), TILE)
            slabs[pl.ds(per * a, per), :, lanes] = tile.astype(jnp.bfloat16).reshape(per, side, TILE)

    def tile_row(i):
        up = jnp.where(i == 0, 1, jnp.where(i == 1, 2, jnp.where(i == 2, 0, 3)))
        return jnp.where(upper == 1, up, 3 - up)

    def send_copy(s, to):
        lanes = pl.ds(pl.multiple_of(s * wide, wide), wide)
        return pltpu.make_async_remote_copy(
            src_ref=slabs.at[to, :, lanes],
            dst_ref=moved.at[me, :, lanes],
            send_sem=send.at[s],
            recv_sem=recv.at[s],
            device_id={"tm": to},
            device_id_type=mesh_id,
        )

    def chunk_wait(s, sem):
        lanes = pl.ds(pl.multiple_of(s * wide, wide), wide)
        taken = moved.at[pl.ds(0, groups - 1), :, lanes]
        pltpu.make_async_copy(taken, taken, sem.at[s]).wait()

    def halo_copy(i):
        source = (rows - MAXSHIFT, 0)[i]
        return pltpu.make_async_remote_copy(
            src_ref=movie_ref.at[pl.ds(source, MAXSHIFT)],
            dst_ref=(before, after)[i],
            send_sem=halo_send.at[i],
            recv_sem=halo_recv.at[i],
            device_id={"pix": (pix + 1, pix - 1)[i]},
            device_id_type=mesh_id,
        )

    sends_halo = (pix < bands - 1, pix > 0)
    gets_halo = (pix > 0, pix < bands - 1)

    side_x = lax.rem(me, per)
    mine = (side_x, per - 1 - side_x)
    outer_z = (1 - upper) * last
    inner_z = 2 - upper
    other_z = jnp.where(inside, upper * last, 1 + upper)
    high_z = jnp.where(upper == 1, inner_z, outer_z)
    low_z = jnp.where(upper == 1, outer_z, inner_z)
    targets = [z * per + x for z in (high_z, low_z) for x in (mine[1], mine[0])]
    targets += [other_z * per + mine[1], quarter * per + mine[1], other_z * per + mine[0]]

    units = across // UNIT
    nearest = tile_row(0)
    enter = jnp.where(quarter == 0, 2 * units, EARLY * wide // (UNIT * TILE))
    widen(0)
    shift_copy.wait()

    @pl.loop(0, 4 * units)
    def _(u):
        @pl.when(u == enter)
        def _():
            pl.semaphore_wait(barrier, jnp.where(inside, per, groups - 1) + bands - 1)
            for i in range(2):

                @pl.when(sends_halo[i])
                def _():
                    halo_copy(i).start()

            @pl.loop(0, EARLY)
            def _(s):
                for e in range(per):
                    send_copy(s, per * nearest + e).start()

            @pl.when(quarter == last)
            def _():
                for q in range(1, last):
                    to = {"tm": q * per + lax.rem(me, per)}
                    pl.semaphore_signal(ready, inc=1, device_id=to, device_id_type=mesh_id)

        @pl.when(u == 1)
        def _():
            widen(1)

        @pl.when(u == 2 * units)
        def _():
            widen(2)
            widen(3)
            for k in range(2):

                @pl.when(gets_halo[k])
                def _():
                    halo_copy(k).wait_recv()

                @pl.when(jnp.logical_not(gets_halo[k]))
                def _():
                    (before, after)[k][...] = jnp.zeros((MAXSHIFT, width), jnp.bfloat16)

            for j in range(across):
                lanes = pl.ds(j * TILE, TILE)
                padded[j + 1, pl.ds(0, MAXSHIFT), :] = before[:, lanes].astype(jnp.float32)
                padded[j + 1, pl.ds(rows + MAXSHIFT, MAXSHIFT), :] = after[:, lanes].astype(jnp.float32)

        @pl.when(u == 2 * units + 2 * (AHEAD * wide // (UNIT * TILE)))
        def _():
            @pl.when(inside)
            def _():
                pl.semaphore_wait(ready, 1)

            @pl.loop(0, AHEAD)
            def _(s):
                for to in targets:

                    @pl.when(jnp.logical_or(s >= EARLY, to // per != nearest))
                    def _():
                        send_copy(s, to).start()

        v = lax.rem(u, 2 * units)
        register_tiles(tile_row(u // (2 * units) * 2 + lax.rem(v, 2)), v // 2)

    own = pltpu.make_async_copy(slabs.at[me], moved.at[me], here)
    own.start()

    @pl.loop(0, steps)
    def _(s):
        feet_copy(s).start()

    sums[...] = jnp.zeros_like(sums)
    for copy in table_copies:
        copy.wait()
    for s in range(steps):
        labels[s] = jnp.concatenate([ids_ref[p : p + 1, :] for p in range(s * GROUP, (s + 1) * GROUP)], axis=1)
    for i in range(2):

        @pl.when(sends_halo[i])
        def _():
            halo_copy(i).wait_send()

    own.wait()

    @pl.loop(0, steps)
    def _(s):
        @pl.when(s + AHEAD < steps)
        def _():
            chunk_wait(s, send)
            for to in targets:
                send_copy(s + AHEAD, to).start()

        feet_copy(s).wait()
        span = turned.shape[1]
        within = labels[s] % local
        places = lax.broadcasted_iota(jnp.int32, (local, span), 0)
        onehot[...] = (places == within).astype(jnp.float32).astype(jnp.bfloat16).T
        for c in range(0, turned.shape[0], span):
            turned[c : c + span, :] = feet[s, :, :, c : c + span].reshape(span, span).T

        chunk_wait(s, recv)
        lanes = pl.ds(pl.multiple_of(s * wide, wide), wide)
        sums[...] += project_step(local, moved[:, :, lanes], turned, labels[s], onehot, row_ref, col_ref, mix_ref)

    frames = groups
    owners = groups * bands
    place = me * bands + pix

    def last_copy(to):
        return pltpu.make_async_remote_copy(
            src_ref=sums.at[pl.ds(pl.multiple_of(to * frames, frames), frames)],
            dst_ref=landed.at[place],
            send_sem=last_send,
            recv_sem=last_recv,
            device_id={"tm": to // bands, "pix": lax.rem(to, bands)},
            device_id_type=mesh_id,
        )

    @pl.loop(0, owners)
    def _(to):
        @pl.when(to != place)
        def _():
            last_copy(to).start()

    landed[place] = sums[pl.ds(pl.multiple_of(place * frames, frames), frames), :]

    @pl.loop(steps - AHEAD, steps)
    def _(s):
        chunk_wait(s, send)

    taken = landed.at[pl.ds(0, owners - 1)]
    pltpu.make_async_copy(taken, taken, last_recv).wait()
    out_ref[...] = jnp.sum(landed[...], axis=0)
    pltpu.make_async_copy(taken, taken, last_send).wait()


def fused(band, shifts, footprints, ids, groups, bands):
    rows, width = band.shape
    frames = groups
    owners = groups * bands
    steps = width // (GROUP * PATCH)
    foot_cols = footprints.shape[1]
    local = NEURONS // owners
    base = gauss_table(PATCH, pixel_sigma)
    time = gauss_table(frames, frame_sigma)
    full = GROUP * PATCH
    eye = np.eye(GROUP, dtype=np.float32)
    row_table = np.kron(eye, base.astype(np.float32)).astype(ml_dtypes.bfloat16)
    col_table = np.kron(eye, base.astype(np.float32).T).astype(ml_dtypes.bfloat16)
    half = full // frames
    spots = np.eye(half, dtype=np.float32)
    keep = np.einsum("gf,rs->rgfs", np.eye(frames, dtype=np.float32), spots)
    blur = np.einsum("gf,rs->rgfs", time.astype(np.float32), spots)
    mix = np.concatenate([keep.reshape(full, full), -blur.reshape(full, full)], axis=1).astype(ml_dtypes.bfloat16)
    hbm = pl.BlockSpec(memory_space=pltpu.HBM)
    tall = rows + 2 * MAXSHIFT
    bf16, f32, dma = jnp.bfloat16, jnp.float32, pltpu.SemaphoreType.DMA
    return pl.pallas_call(
        lambda *refs: fused_kernel(local, *refs),
        out_shape=jax.ShapeDtypeStruct((frames, local), f32),
        in_specs=[hbm] * 7,
        out_specs=pl.BlockSpec(memory_space=pltpu.VMEM),
        scratch_shapes=[
            pltpu.SMEM(shifts.shape, jnp.int32),
            pltpu.VMEM(ids.shape, jnp.int32),
            pltpu.VMEM((rows, width), bf16),
            pltpu.VMEM((MAXSHIFT, width), bf16),
            pltpu.VMEM((MAXSHIFT, width), bf16),
            pltpu.VMEM((width // TILE + 2, tall, TILE), f32),
            pltpu.VMEM((groups, PATCH, width), bf16),
            pltpu.VMEM((groups, PATCH, width), bf16),
            pltpu.VMEM((steps, GROUP, foot_cols, PATCH * PATCH), bf16),
            pltpu.VMEM((PATCH * PATCH, GROUP * foot_cols), bf16),
            pltpu.VMEM((GROUP * foot_cols, local), bf16),
            pltpu.VMEM(row_table.shape, bf16),
            pltpu.VMEM(col_table.shape, bf16),
            pltpu.VMEM(mix.shape, bf16),
            pltpu.VMEM((steps, 1, GROUP * foot_cols), jnp.int32),
            pltpu.VMEM((owners * frames, local), f32),
            pltpu.VMEM((owners, frames, local), f32),
            dma((4,)),
            dma((5,)),
            dma((steps,)),
            dma((2,)),
            dma((2,)),
            dma((steps,)),
            dma((steps,)),
            dma,
            dma,
            dma,
            pltpu.SemaphoreType.REGULAR,
        ],
        compiler_params=pltpu.CompilerParams(
            vmem_limit_bytes=48 << 20, collective_id=0, has_side_effects=True
        ),
        name="fused",
    )(
        *(
            pltpu.with_memory_space_constraint(operand, pltpu.HBM)
            for operand in (
                shifts,
                band,
                footprints,
                ids,
                jnp.asarray(row_table),
                jnp.asarray(col_table),
                jnp.asarray(mix),
            )
        )
    )


def project_general(moved, footprints, labels, owners):
    frames, side, width = moved.shape
    base = jnp.asarray(gauss_table(side, pixel_sigma))
    time = jnp.asarray(gauss_table(frames, frame_sigma))
    blocks = moved.reshape(frames, side, width // side, side)
    dot = lambda spec, a, b: jnp.einsum(spec, a, b, preferred_element_type=jnp.float32)
    along_rows = dot("ij,fjpc->fipc", base, blocks).astype(jnp.bfloat16)
    along_cols = dot("fipc,dc->fipd", along_rows, base).astype(jnp.bfloat16)
    clean = (blocks.astype(jnp.float32) - dot("gf,fipc->gipc", time, along_cols)).astype(jnp.bfloat16)
    pixels = clean.transpose(2, 0, 1, 3).reshape(width // side, frames, side * side)
    partial = dot("pfx,pkx->fpk", pixels, footprints).reshape(frames, -1)
    wanted = jnp.arange(NEURONS, dtype=jnp.int32)
    onehot = (labels.reshape(-1)[:, None] == wanted[None, :]).astype(jnp.float32)
    sums = jnp.dot(partial, onehot, precision=lax.Precision.HIGHEST, preferred_element_type=jnp.float32)
    return sums.reshape(frames, owners, -1).transpose(1, 0, 2).reshape(owners * frames, -1)


def on_device(movie, shifts, footprints, neuron_ids):
    band = movie[0]
    rows, width = band.shape
    groups = lax.axis_size("tm")
    bands = lax.axis_size("pix")
    owners = groups * bands
    wide = footprints.shape[1] * PATCH
    frames = groups * movie.shape[0]
    fits = (
        frames == groups
        and rows == 4 * TILE
        and rows == groups * PATCH
        and frames * 32 == GROUP * PATCH
        and wide == width
        and NEURONS // owners == LANES
    )
    if fits:
        return fused(band, shifts[0].transpose(0, 2, 1), footprints[0], neuron_ids[0], groups, bands).T
    before, after = halo(band)
    registered = register(band, before, after, shifts)
    slabs = registered.reshape(rows // PATCH, PATCH, width // wide, wide)
    slabs = slabs.transpose(0, 2, 1, 3).reshape(groups, PATCH, wide)
    moved = lax.all_to_all(slabs, "tm", split_axis=0, concat_axis=0, tiled=True)
    sums = project_general(moved, footprints[0], neuron_ids[0], owners)
    sums = lax.all_to_all(
        sums.reshape(owners, frames, -1), ("tm", "pix"), split_axis=0, concat_axis=0, tiled=True
    )
    return jnp.sum(sums, axis=0).T


def solution(mesh):
    in_specs = (
        P("tm", "pix", None),
        P("tm", "pix", None, None),
        P("pix", "tm", None, None),
        P("pix", "tm", None),
    )
    out_specs = P(("tm", "pix"), None)
    return jax.shard_map(
        on_device, mesh=mesh, in_specs=in_specs, out_specs=out_specs, check_vma=False
    )
```
